512 devices in a mesh: seq: 64 (over z, x, core), head: 8 (over y).
Axes of the slice: x: 4, y: 8, z: 8, core: 2. Of those that a mesh axis runs over, the one named last changes fastest.
Arguments:
- query: bfloat16 [16384, 4096], P(('seq', 'head')), may hold values from -6 to 6
- key_in: bfloat16 [16384, 4096], P(('seq', 'head')), may hold values from -6 to 6
- value: bfloat16 [16384, 4096], P(('seq', 'head')), may hold values from -6 to 6
- out_grad: bfloat16 [16384, 4096], P(('seq', 'head')), may hold values from -6 to 6
- block_keep: int32 [128], replicated, may hold values from 0 to 1, as said below
- strided_pick: int32 [128, 2], replicated, may hold values from 1 to 4, as said below
- summary_cols: int32 [128, 8], replicated, may hold values from 0 to 127, as said below
Outputs:
- attended: bfloat16 [16384, 4096], P(('seq', 'head'))
- grad_query: bfloat16 [16384, 4096], P(('seq', 'head'))
- grad_key: bfloat16 [16384, 4096], P(('seq', 'head'))
- grad_value: bfloat16 [16384, 4096], P(('seq', 'head'))
The draws below stay inside these ranges and needn't reach their ends.
Inputs may be any that keep to these rules, and one draw needn't show every extreme that they name: `block_keep`: exactly one run of consecutive blocks, 8 to 32 blocks long, holds 0; every other block holds 1. `strided_pick`: the two entries of a row differ. `summary_cols`: entry c of each row lies in c * (16) to (c + 1) * 16 - 1.
All inputs are finite; a program needn't handle non-finite values.
Results may differ from the reference program's by a relative error of at most 0.034.
Values may be sent and summed in bfloat16 or wider, within the bound.
No kernel may reach another device: no remote copies, remote signals or barrier semaphores. Data moves between devices by JAX's collectives and lax.ppermute only.
A program may use at most 64 MiB of HBM per device.

```python
import math
import jax
import jax.numpy as jnp
from jax import lax

H = 32
HD = 128
BLK = 128
SUMMARY = 8
CANDS = 4
DM = 4096
SEQ = 16384
NB = 128


def paired_rows(key):
    base = jax.random.fold_in(key, 17)
    parts = jax.random.split(base, 2)
    key_rows = jax.random.truncated_normal(parts[0], -4.0, 4.0, (SEQ, DM), jnp.float32)
    query_rows = jax.random.truncated_normal(parts[1], -4.0, 4.0, (SEQ, DM), jnp.float32)
    return (query_rows, key_rows)


def draw_query(key, part):
    return paired_rows(key)[0].astype(jnp.bfloat16)


def draw_key_in(key, part):
    return paired_rows(key)[1].astype(jnp.bfloat16)


def draw_block_keep(key, part):
    parts = jax.random.split(jax.random.fold_in(key, 3), 2)
    length = jax.random.randint(parts[0], (), NB // 16, NB // 4 + 1)
    start = jax.random.randint(parts[1], (), 0, NB - length + 1)
    block_ids = jnp.arange(NB, dtype=jnp.int32)
    return jnp.where((block_ids >= start) & (block_ids < start + length), 0, 1).astype(jnp.int32)


def draw_strided_pick(key, part):
    parts = jax.random.split(jax.random.fold_in(key, 5), 2)
    leading = jax.random.randint(parts[0], (NB, 1), 1, CANDS + 1)
    offset = jax.random.randint(parts[1], (NB, 1), 1, CANDS)
    trailing = 1 + (leading - 1 + offset) % CANDS
    return jnp.concatenate([leading, trailing], axis=1).astype(jnp.int32)


def draw_summary_cols(key, part):
    spread = BLK // SUMMARY
    offsets = jax.random.randint(jax.random.fold_in(key, 7), (NB, SUMMARY), 0, spread)
    return (jnp.arange(SUMMARY, dtype=jnp.int32)[None, :] * spread + offsets).astype(jnp.int32)


def levels(stream_key, shape, pieces, low, top_value):
    loudness, own = 1.0, jax.random.fold_in(stream_key, 6)
    for dim, shards_of in pieces:
        steps = jnp.exp(jax.random.uniform(jax.random.fold_in(own, dim), (shards_of,), jnp.float32, low / len(pieces), top_value / len(pieces)))
        loudness = loudness * jnp.repeat(steps, shape[dim] // shards_of).reshape([-1 if axis == dim else 1 for axis in range(len(shape))])
    return loudness


def bell_draw(stream_key, extent, scale, limit, cuts=(), kind=jnp.bfloat16):
    array = scale * jax.random.normal(stream_key, extent, jnp.float32)
    if cuts:
        array = array * levels(stream_key, extent, cuts, -0.22, 0.18)
    return jnp.clip(array, -limit, limit).astype(kind)


def setup_inputs(seed: int = 0) -> dict:
    key_list = jax.random.split(jax.random.key(seed), 8)
    return {
        "query": draw_query(jax.random.fold_in(key_list[7], 71), 0),
        "key_in": draw_key_in(jax.random.fold_in(key_list[7], 71), 0),
        "value": bell_draw(key_list[2], (SEQ, DM), 1.0, 6.0, ((0, 512),)),
        "out_grad": bell_draw(key_list[3], (SEQ, DM), 1.0, 6.0, ((0, 512),)),
        "block_keep": draw_block_keep(jax.random.fold_in(key_list[7], 71), 0),
        "strided_pick": draw_strided_pick(jax.random.fold_in(key_list[7], 71), 0),
        "summary_cols": draw_summary_cols(jax.random.fold_in(key_list[7], 71), 0),
    }


def attend(queries, cotangent, key_rows, values, allowed, alive):
    scaling = 1.0 / math.sqrt(HD)
    scores = jnp.einsum('qhd,khd->hqk', queries.astype(jnp.float32), key_rows.astype(jnp.float32)) * scaling
    allow_all = allowed[None, :, :]
    masked = jnp.where(allow_all, scores, -jnp.inf)
    row_max = lax.optimization_barrier(jnp.max(masked, axis=2, keepdims=True))
    log_total = row_max + jnp.log(lax.optimization_barrier(jnp.sum(jnp.exp(masked - row_max), axis=2, keepdims=True)))
    weights = jnp.where(allow_all, jnp.exp(scores - log_total), 0.0) * alive
    weights_low = weights.astype(jnp.bfloat16)
    attended = jnp.einsum('hqk,khd->qhd', weights_low.astype(jnp.float32), values.astype(jnp.float32)).astype(jnp.bfloat16)
    correction = lax.optimization_barrier(jnp.sum(cotangent.astype(jnp.float32) * attended.astype(jnp.float32), axis=2))
    weight_grad = jnp.einsum('qhd,khd->hqk', cotangent.astype(jnp.float32), values.astype(jnp.float32))
    score_grad = (weights * (weight_grad - jnp.transpose(correction)[:, :, None]) * scaling).astype(jnp.bfloat16)
    query_grad = jnp.einsum('hqk,khd->qhd', score_grad.astype(jnp.float32), key_rows.astype(jnp.float32)).astype(jnp.bfloat16)
    key_grad = jnp.einsum('hqk,qhd->khd', score_grad.astype(jnp.float32), queries.astype(jnp.float32))
    value_grad = jnp.einsum('hqk,qhd->khd', weights_low.astype(jnp.float32), cotangent.astype(jnp.float32))
    return (attended, query_grad, key_grad, value_grad)

def split_kinds(source):
    shaped = source.reshape(SEQ, H // 4, 2, 2, HD)
    block_count = SEQ // BLK
    fixed = shaped[:, :, 0].reshape(block_count, BLK, H // 2, HD)
    strided = shaped[:, :, 1].reshape(block_count, BLK, H // 2, HD)
    return (fixed, strided)

def join_kinds(fixed, strided):
    fixed_rows = fixed.reshape(SEQ, H // 4, 2, HD)
    strided_rows = strided.reshape(SEQ, H // 4, 2, HD)
    return jnp.stack([fixed_rows, strided_rows], axis=2).reshape(SEQ, H * HD)

def fixed_part(queries, key_rows, values, cotangent, summary_cols, block_keep):
    block_count = SEQ // BLK
    head_count = H // 2
    positions = summary_cols[:, :, None, None]
    summary_k = jnp.take_along_axis(key_rows, positions, axis=1).reshape(block_count * SUMMARY, head_count, HD)
    summary_v = jnp.take_along_axis(values, positions, axis=1).reshape(block_count * SUMMARY, head_count, HD)
    causal = jnp.arange(BLK)[:, None] >= jnp.arange(BLK)[None, :]
    block_ids = jnp.arange(block_count, dtype=jnp.int32)
    keeping = block_keep == 1

    def visit_block(totals, inputs):
        sum_keys, sum_values = totals
        q_block, k_block, v_block, g_block, current = inputs
        earlier = (block_ids < current) & keeping
        far_allowed = jnp.broadcast_to(earlier[:, None], (block_count, SUMMARY)).reshape(block_count * SUMMARY)
        allowed = jnp.concatenate([causal, jnp.broadcast_to(far_allowed[None, :], (BLK, block_count * SUMMARY))], axis=1)
        alive = jnp.sum(jnp.where(block_ids == current, block_keep, 0)).astype(jnp.float32)
        attended, query_grad, key_grad, value_grad = attend(q_block, g_block, jnp.concatenate([k_block, summary_k]), jnp.concatenate([v_block, summary_v]), allowed, alive)
        return ((sum_keys + key_grad[BLK:], sum_values + value_grad[BLK:]), (attended, query_grad, key_grad[:BLK], value_grad[:BLK]))
    empty_sum = jnp.zeros((block_count * SUMMARY, head_count, HD), jnp.float32)
    totals, stacked = lax.scan(visit_block, (empty_sum, empty_sum), (queries, key_rows, values, cotangent, block_ids))
    placing = (jnp.arange(BLK, dtype=jnp.int32)[None, None, :] == summary_cols[:, :, None]).astype(jnp.float32)
    key_grad = stacked[2] + jnp.einsum('bcp,bchd->bphd', placing, totals[0].reshape(block_count, SUMMARY, head_count, HD), precision=lax.Precision.HIGHEST)
    value_grad = stacked[3] + jnp.einsum('bcp,bchd->bphd', placing, totals[1].reshape(block_count, SUMMARY, head_count, HD), precision=lax.Precision.HIGHEST)
    return (stacked[0], stacked[1], key_grad.astype(jnp.bfloat16), value_grad.astype(jnp.bfloat16))

def strided_part(queries, key_rows, values, cotangent, strided_pick, block_keep):
    block_count = SEQ // BLK
    head_count = H // 2
    stride_blocks = block_count // 8
    multiples = jnp.arange(1, CANDS + 1, dtype=jnp.int32)
    causal = jnp.arange(BLK)[:, None] >= jnp.arange(BLK)[None, :]
    block_ids = jnp.arange(block_count, dtype=jnp.int32)

    def visit_block(totals, inputs):
        sum_keys, sum_values = totals
        q_block, k_block, v_block, g_block, chosen, current = inputs
        candidates = current - stride_blocks * multiples
        clipped = jnp.maximum(candidates, 0).astype(jnp.int32)
        picked = jnp.any(chosen[None, :] == multiples[:, None], axis=1)
        usable = (candidates >= 0) & picked & (block_keep[clipped] == 1)
        far_allowed = jnp.broadcast_to(usable[:, None], (CANDS, BLK)).reshape(CANDS * BLK)
        allowed = jnp.concatenate([causal, jnp.broadcast_to(far_allowed[None, :], (BLK, CANDS * BLK))], axis=1)
        alive = jnp.sum(jnp.where(block_ids == current, block_keep, 0)).astype(jnp.float32)
        far_keys = key_rows[clipped].reshape(CANDS * BLK, head_count, HD)
        far_values = values[clipped].reshape(CANDS * BLK, head_count, HD)
        attended, query_grad, key_grad, value_grad = attend(q_block, g_block, jnp.concatenate([k_block, far_keys]), jnp.concatenate([v_block, far_values]), allowed, alive)
        sum_keys = sum_keys.at[clipped].add(key_grad[BLK:].reshape(CANDS, BLK, head_count, HD))
        sum_values = sum_values.at[clipped].add(value_grad[BLK:].reshape(CANDS, BLK, head_count, HD))
        sum_keys = sum_keys.at[current].add(key_grad[:BLK])
        sum_values = sum_values.at[current].add(value_grad[:BLK])
        return ((sum_keys, sum_values), (attended, query_grad))
    empty_sum = jnp.zeros((block_count, BLK, head_count, HD), jnp.float32)
    totals, stacked = lax.scan(visit_block, (empty_sum, empty_sum), (queries, key_rows, values, cotangent, strided_pick, block_ids))
    return (stacked[0], stacked[1], totals[0].astype(jnp.bfloat16), totals[1].astype(jnp.bfloat16))

def reference(query, key_in, value, out_grad, block_keep, strided_pick, summary_cols):
    q_fixed, q_strided = split_kinds(query)
    k_fixed, k_strided = split_kinds(key_in)
    v_fixed, v_strided = split_kinds(value)
    g_fixed, g_strided = split_kinds(out_grad)
    fixed = fixed_part(q_fixed, k_fixed, v_fixed, g_fixed, summary_cols, block_keep)
    strided = strided_part(q_strided, k_strided, v_strided, g_strided, strided_pick, block_keep)
    return (join_kinds(fixed[0], strided[0]), join_kinds(fixed[1], strided[1]), join_kinds(fixed[2], strided[2]), join_kinds(fixed[3], strided[3]))
```

```python
import math

import jax
import jax.numpy as jnp
import numpy as np
from jax import lax
from jax.experimental import pallas as pl
from jax.experimental.pallas import tpu as pltpu
from jax.sharding import Mesh
from jax.sharding import PartitionSpec as P

HD = 128
BLK = 128
SUMMARY = 8
CANDS = 4
ROWS = 32
SCALE = 1.0 / math.sqrt(HD)
LOG2 = SCALE * math.log2(math.e)
NEG = -1e30

AXES = ("z", "x", "c", "h", "q")
NEAR = ("c", "h", "q")
FAR = ("z", "x")

F32 = jnp.float32
BF16 = jnp.bfloat16

VMEM = pl.BlockSpec(memory_space=pltpu.VMEM)
SMEM = pl.BlockSpec(memory_space=pltpu.SMEM)
PARAMS = pltpu.CompilerParams(vmem_limit_bytes=56 * 1024 * 1024)


def dot(a, b, dims):
    return lax.dot_general(a, b, (dims, ((), ())), preferred_element_type=F32)


def dot_nt(a, b):
    return dot(a, b, ((1,), (1,)))


def dot_nn(a, b):
    return dot(a, b, ((1,), (0,)))


def dot_tn(a, b):
    return dot(a, b, ((0,), (0,)))


def fixed_head(d):
    return (d // 2) * 4 + d % 2


def strided_head(d):
    return (d // 2) * 4 + 2 + d % 2


def call(body, out_shape, specs, scratch=()):
    return pl.pallas_call(
        body,
        out_shape=out_shape,
        in_specs=specs,
        out_specs=jax.tree.map(lambda _: VMEM, out_shape),
        scratch_shapes=list(scratch),
        compiler_params=PARAMS,
    )


def causal_mask():
    rows = lax.broadcasted_iota(jnp.int32, (BLK, BLK), 0)
    cols = lax.broadcasted_iota(jnp.int32, (BLK, BLK), 1)
    return rows >= cols


def pack_body(q_ref, k_ref, v_ref, g_ref, s_ref, f_ref):
    for a, ref in enumerate((q_ref, k_ref, v_ref, g_ref)):
        for d in range(16):
            hs, hf = strided_head(d), fixed_head(d)
            s_ref[d, a * ROWS : (a + 1) * ROWS, :] = ref[:, hs * HD : (hs + 1) * HD]
            f_ref[d, a * ROWS : (a + 1) * ROWS, :] = ref[:, hf * HD : (hf + 1) * HD]


def pack(q, k, v, g):
    shape = jax.ShapeDtypeStruct((16, 4 * ROWS, HD), BF16)
    return call(pack_body, (shape, shape), [VMEM] * 4)(q, k, v, g)


def block_of(ref, j, a):
    return ref[4 * j : 4 * j + 4, a * ROWS : (a + 1) * ROWS, :].reshape(BLK, HD)


def summary_body(meta_ref, cols_ref, x_ref, out_ref):
    first = meta_ref[2]
    row = lax.broadcasted_iota(jnp.int32, (4 * SUMMARY, HD), 0)
    lane = lax.broadcasted_iota(jnp.int32, (4 * SUMMARY, HD), 1)
    target = jnp.zeros((4 * SUMMARY, HD), jnp.int32)
    for j in range(4):
        for c in range(SUMMARY):
            target = jnp.where(row == j * SUMMARY + c, cols_ref[first + j, c] + j * BLK, target)
    ks = jnp.zeros((4 * SUMMARY, HD), F32)
    vs = jnp.zeros((4 * SUMMARY, HD), F32)
    for j in range(4):
        one = (target == lane + j * BLK).astype(F32).astype(BF16)
        ks = ks + dot_nn(one, block_of(x_ref, j, 1))
        vs = vs + dot_nn(one, block_of(x_ref, j, 2))
    ks = ks.astype(BF16)
    vs = vs.astype(BF16)
    for i in range(32):
        out_ref[i, 0:32, :] = ks
        out_ref[i, 32:64, :] = vs


def summary(meta, cols, x):
    shape = jax.ShapeDtypeStruct((32, 64, HD), BF16)
    return call(summary_body, shape, [SMEM, SMEM, VMEM])(meta, cols, x)


def fixed_body(meta_ref, keep_ref, bias_ref, x_ref, g_ref, oq_ref, own_ref, rs_ref, p_sc, d_sc):
    first = meta_ref[2]
    causal = causal_mask()
    far = 128 * SUMMARY
    col_block = lax.broadcasted_iota(jnp.int32, (1, far), 1) >> 3
    bias_keep = bias_ref[...]
    ks = g_ref[:, 0:32, :].reshape(far, HD)
    vs = g_ref[:, 32:64, :].reshape(far, HD)
    for j in range(4):
        q = block_of(x_ref, j, 0)
        k = block_of(x_ref, j, 1)
        v = block_of(x_ref, j, 2)
        g = block_of(x_ref, j, 3)
        current = first + j
        alive = keep_ref[current].astype(F32)
        bias = jnp.where(col_block < current, bias_keep, NEG)
        t_far = dot_nt(q, ks) * LOG2 + bias
        t_own = jnp.where(causal, dot_nt(q, k) * LOG2, NEG)
        top = jnp.maximum(
            jnp.max(t_far, axis=1, keepdims=True), jnp.max(t_own, axis=1, keepdims=True)
        )
        p_far = jnp.exp2(t_far - top)
        p_own = jnp.exp2(t_own - top)
        total = jnp.sum(p_far, axis=1, keepdims=True) + jnp.sum(p_own, axis=1, keepdims=True)
        inv = alive / total
        p_far = p_far * inv
        p_own = p_own * inv
        pl_far = p_far.astype(BF16)
        pl_own = p_own.astype(BF16)
        out = (dot_nn(pl_far, vs) + dot_nn(pl_own, v)).astype(BF16)
        delta = jnp.sum(g.astype(F32) * out.astype(F32), axis=1, keepdims=True)
        ds_far = (p_far * (dot_nt(g, vs) - delta) * SCALE).astype(BF16)
        ds_own = (p_own * (dot_nt(g, v) - delta) * SCALE).astype(BF16)
        dq = (dot_nn(ds_far, ks) + dot_nn(ds_own, k)).astype(BF16)
        oq_ref[4 * j : 4 * j + 4, 0:ROWS, :] = out.reshape(4, ROWS, HD)
        oq_ref[4 * j : 4 * j + 4, ROWS : 2 * ROWS, :] = dq.reshape(4, ROWS, HD)
        own_ref[0, j * BLK : (j + 1) * BLK, :] = dot_tn(ds_own, q)
        own_ref[1, j * BLK : (j + 1) * BLK, :] = dot_tn(pl_own, g)
        p_sc[j * BLK : (j + 1) * BLK, :] = pl_far
        d_sc[j * BLK : (j + 1) * BLK, :] = ds_far
    q_all = x_ref[:, 0:ROWS, :].reshape(4 * BLK, HD)
    g_all = x_ref[:, 3 * ROWS : 4 * ROWS, :].reshape(4 * BLK, HD)
    rs_ref[:, 0:32, :] = dot_tn(d_sc[...], q_all).astype(BF16).reshape(32, 32, HD)
    rs_ref[:, 32:64, :] = dot_tn(p_sc[...], g_all).astype(BF16).reshape(32, 32, HD)


def fixed(meta, keep, bias, x, g):
    shapes = (
        jax.ShapeDtypeStruct((16, 2 * ROWS, HD), BF16),
        jax.ShapeDtypeStruct((2, 4 * BLK, HD), F32),
        jax.ShapeDtypeStruct((32, 64, HD), BF16),
    )
    scratch = [pltpu.VMEM((4 * BLK, 128 * SUMMARY), BF16)] * 2
    return call(fixed_body, shapes, [SMEM, SMEM, VMEM, VMEM, VMEM], scratch)(
        meta, keep, bias, x, g
    )


def strided_body(meta_ref, keep_ref, pick_ref, x_ref, out_ref, dk_sc, dv_sc):
    z = meta_ref[0]
    x = meta_ref[1]
    causal = causal_mask()

    def load(zz, j, a):
        return x_ref[zz, pl.ds(4 * j, 4), a * ROWS : (a + 1) * ROWS, :].reshape(BLK, HD)

    def store(j, a, value):
        out_ref[pl.ds(4 * j, 4), a * ROWS : (a + 1) * ROWS, :] = value.astype(BF16).reshape(
            4, ROWS, HD
        )

    def forward(zz, j):
        block = zz * 16 + x * 4 + j
        q = load(zz, j, 0)
        g = load(zz, j, 3)
        at = []
        scores = [jnp.where(causal, dot_nt(q, load(zz, j, 1)) * LOG2, NEG)]
        for slot in range(2):
            behind = zz - pick_ref[block, slot]
            clipped = jnp.maximum(behind, 0)
            kept = keep_ref[clipped * 16 + x * 4 + j] == 1
            bias = jnp.where((behind >= 0) & kept, 0.0, NEG)
            at.append(clipped)
            scores.append(dot_nt(q, load(clipped, j, 1)) * LOG2 + bias)
        top = jnp.maximum(
            jnp.maximum(
                jnp.max(scores[0], axis=1, keepdims=True),
                jnp.max(scores[1], axis=1, keepdims=True),
            ),
            jnp.max(scores[2], axis=1, keepdims=True),
        )
        weights = [jnp.exp2(s - top) for s in scores]
        total = sum(jnp.sum(w, axis=1, keepdims=True) for w in weights)
        inv = keep_ref[block].astype(F32) / total
        weights = [w * inv for w in weights]
        low = [w.astype(BF16) for w in weights]
        out = dot_nn(low[0], load(zz, j, 2))
        for slot in range(2):
            out = out + dot_nn(low[slot + 1], load(at[slot], j, 2))
        out = out.astype(BF16)
        delta = jnp.sum(g.astype(F32) * out.astype(F32), axis=1, keepdims=True)
        return q, g, at, weights, low, out, delta

    def one_block(j, carry):
        q, g, at, weights, low, out, delta = forward(z, j)
        store(j, 0, out)
        rows = [z] + at
        dq = jnp.zeros((BLK, HD), F32)
        for i in range(3):
            ds = (weights[i] * (dot_nt(g, load(rows[i], j, 2)) - delta) * SCALE).astype(BF16)
            dq = dq + dot_nn(ds, load(rows[i], j, 1))
            if i == 0:
                dk_sc[...] = dot_tn(ds, q)
                dv_sc[...] = dot_tn(low[0], g)
        store(j, 1, dq)
        mine = keep_ref[z * 16 + x * 4 + j] == 1
        for m in range(1, CANDS + 1):
            later = jnp.minimum(z + m, 7)
            block = later * 16 + x * 4 + j
            reads = (pick_ref[block, 0] == m) | (pick_ref[block, 1] == m)

            @pl.when((z + m <= 7) & reads & mine & (keep_ref[block] == 1))
            def _():
                q2, g2, _, w2, low2, _, delta2 = forward(later, j)
                second = pick_ref[block, 1] == m
                w = jnp.where(second, w2[2], w2[1])
                w_low = w.astype(BF16)
                ds = (w * (dot_nt(g2, load(z, j, 2)) - delta2) * SCALE).astype(BF16)
                dk_sc[...] += dot_tn(ds, q2)
                dv_sc[...] += dot_tn(w_low, g2)

        store(j, 2, dk_sc[...])
        store(j, 3, dv_sc[...])
        return carry

    lax.fori_loop(0, 4, one_block, 0)


def strided(meta, keep, pick, x):
    shape = jax.ShapeDtypeStruct((16, 4 * ROWS, HD), BF16)
    scratch = [pltpu.VMEM((BLK, HD), F32)] * 2
    return call(strided_body, shape, [SMEM, SMEM, SMEM, VMEM], scratch)(meta, keep, pick, x)


def combine_body(meta_ref, cols_ref, r_ref, own_ref, oq_ref, st_ref, out_ref):
    first = meta_ref[2]
    total = r_ref[0].astype(F32)
    for i in range(1, 32):
        total = total + r_ref[i].astype(F32)
    row = lax.broadcasted_iota(jnp.int32, (16, HD), 0)
    for j in range(4):
        for c in range(SUMMARY):
            at = cols_ref[first + j, c] - 16 * c
            d = 4 * j + c // 2
            low = 16 * (c % 2)
            for a in range(2):
                own = own_ref[a, j * BLK + 16 * c : j * BLK + 16 * (c + 1), :]
                i = a * 32 + j * SUMMARY + c
                extra = jnp.broadcast_to(total[i : i + 1, :], (16, HD))
                value = own + jnp.where(row == at, extra, 0.0)
                base = (2 + a) * ROWS + low
                out_ref[d, base : base + 16, :] = value.astype(BF16)
    for d in range(16):
        out_ref[d, 0 : 2 * ROWS, :] = oq_ref[d]
        out_ref[d, 4 * ROWS : 8 * ROWS, :] = st_ref[d]


def combine(meta, cols, r, own, oq, st):
    shape = jax.ShapeDtypeStruct((16, 8 * ROWS, HD), BF16)
    return call(combine_body, shape, [SMEM, SMEM, VMEM, VMEM, VMEM, VMEM])(
        meta, cols, r, own, oq, st
    )


def unpack_body(x_ref, *outs):
    for a, ref in enumerate(outs):
        for d in range(16):
            hs, hf = strided_head(d), fixed_head(d)
            ref[:, hf * HD : (hf + 1) * HD] = x_ref[d, a * ROWS : (a + 1) * ROWS, :]
            ref[:, hs * HD : (hs + 1) * HD] = x_ref[d, (4 + a) * ROWS : (5 + a) * ROWS, :]


def unpack(x):
    shape = jax.ShapeDtypeStruct((ROWS, 32 * HD), BF16)
    return call(unpack_body, (shape,) * 4, [VMEM])(x)


def exchange(block, axes):
    return lax.all_to_all(block, axes, split_axis=0, concat_axis=0, tiled=True)


def shards(query, key_in, value, out_grad, block_keep, strided_pick, summary_cols):
    z = lax.axis_index("z").astype(jnp.int32)
    x = lax.axis_index("x").astype(jnp.int32)
    meta = jnp.stack([z, x, z * 16 + x * 4])
    bias = jnp.where(jnp.repeat(block_keep, SUMMARY) == 1, 0.0, NEG).astype(F32)[None, :]
    send_s, send_f = pack(query, key_in, value, out_grad)
    got_s = exchange(send_s, NEAR)
    column = lax.all_gather(got_s.reshape(16 * 4 * ROWS, HD), "z", axis=0, tiled=True)
    send_f, got_s = lax.optimization_barrier((send_f, got_s))
    got_f = exchange(send_f, NEAR)
    far = exchange(summary(meta, summary_cols, got_f), FAR)
    oq, own, partial = fixed(meta, block_keep, bias, got_f, far)
    returned = exchange(partial, FAR)
    column, oq = lax.optimization_barrier((column, oq))
    st = strided(meta, block_keep, strided_pick, column.reshape(8, 16, 4 * ROWS, HD))
    back = exchange(combine(meta, summary_cols, returned, own, oq, st), NEAR)
    return tuple(unpack(back))


def solution(mesh):
    split = Mesh(np.asarray(mesh.devices).reshape(8, 4, 2, 2, 4), AXES)
    tokens = P(AXES, None)
    return jax.shard_map(
        shards,
        mesh=split,
        in_specs=(tokens, tokens, tokens, tokens, P(), P(), P()),
        out_specs=(tokens, tokens, tokens, tokens),
        check_vma=False,
    )
```

```python
import math

import jax
import jax.numpy as jnp
import numpy as np
from jax import lax
from jax.experimental import pallas as pl
from jax.experimental.pallas import tpu as pltpu
from jax.sharding import Mesh
from jax.sharding import PartitionSpec as P

HD = 128
BLK = 128
SUMMARY = 8
ROWS = 32
HEADS = 32
RUN = 8
SCALE = 1.0 / math.sqrt(HD)
LOG2 = SCALE * math.log2(math.e)
NEG = -1e30

AXES = ("z", "x", "c", "h", "q")
GROUP = ("z", "q")

F32 = jnp.float32
BF16 = jnp.bfloat16

VMEM = pl.BlockSpec(memory_space=pltpu.VMEM)
SMEM = pl.BlockSpec(memory_space=pltpu.SMEM)
PARAMS = pltpu.CompilerParams(vmem_limit_bytes=56 * 1024 * 1024)


def dot(a, b, dims):
    return lax.dot_general(a, b, (dims, ((), ())), preferred_element_type=F32)


def dot_nt(a, b):
    return dot(a, b, ((1,), (1,)))


def dot_nn(a, b):
    return dot(a, b, ((1,), (0,)))


def dot_tn(a, b):
    return dot(a, b, ((0,), (0,)))


def row_max(a):
    return jnp.max(a, axis=1, keepdims=True)


def row_sum(a):
    return jnp.sum(a, axis=1, keepdims=True)


def shape(*dims, dtype=BF16):
    return jax.ShapeDtypeStruct(dims, dtype)


def call(body, out_shape, specs, scratch=()):
    return pl.pallas_call(
        body,
        out_shape=out_shape,
        in_specs=specs,
        out_specs=jax.tree.map(lambda _: VMEM, out_shape),
        scratch_shapes=list(scratch),
        compiler_params=PARAMS,
    )


def pack_body(a_ref, b_ref, out_ref):
    for i, ref in enumerate((a_ref, b_ref)):
        for d in range(HEADS):
            out_ref[d, i * ROWS : (i + 1) * ROWS, :] = ref[:, d * HD : (d + 1) * HD]


def pack(a, b):
    return call(pack_body, shape(HEADS, 2 * ROWS, HD), [VMEM, VMEM])(a, b)


def unpack_body(x_ref, a_ref, b_ref):
    for i, ref in enumerate((a_ref, b_ref)):
        for d in range(HEADS):
            ref[:, d * HD : (d + 1) * HD] = x_ref[d, i * ROWS : (i + 1) * ROWS, :]


def unpack(x):
    return call(unpack_body, (shape(ROWS, HEADS * HD),) * 2, [VMEM])(x)


def block_of(ref, zz, a):
    return ref[4 * zz : 4 * zz + 4, a * ROWS : (a + 1) * ROWS, :].reshape(BLK, HD)


def summary_body(meta_ref, cols_ref, kv_ref, out_ref):
    residue = meta_ref[1] * 4 + meta_ref[2] * 2 + meta_ref[3]
    row = lax.broadcasted_iota(jnp.int32, (16, BLK), 0)
    lane = lax.broadcasted_iota(jnp.int32, (16, BLK), 1)
    for pair in range(4):
        rows = [jnp.zeros((16, HD), F32) for _ in range(2)]
        for half in range(2):
            zz = 2 * pair + half
            target = jnp.full((16, BLK), -1, jnp.int32)
            for c in range(SUMMARY):
                target = jnp.where(row == half * SUMMARY + c, cols_ref[zz * 16 + residue, c], target)
            one = (target == lane).astype(F32).astype(BF16)
            for a in range(2):
                rows[a] = rows[a] + dot_nn(one, block_of(kv_ref, zz, a))
        for a in range(2):
            out_ref[a * 64 + pair * 16 : a * 64 + (pair + 1) * 16, :] = rows[a].astype(BF16)


def summary(meta, cols, kv):
    return call(summary_body, shape(128, HD), [SMEM, SMEM, VMEM])(meta, cols, kv)


def fixed_head(meta_ref, kv_ref, qg_ref, parts, oq_ref, dkv_ref, outs, k_sc, v_sc, p_sc, d_sc):
    x, c, h = meta_ref[1], meta_ref[2], meta_ref[3]
    gone, back = meta_ref[5], meta_ref[6]
    residue = x * 4 + c * 2 + h
    causal = lax.broadcasted_iota(jnp.int32, (BLK, BLK), 0) >= lax.broadcasted_iota(
        jnp.int32, (BLK, BLK), 1
    )
    for pair in range(4):
        for rel in range(16):
            at = pair * 256 + rel * 16
            ref = parts[rel // 4]
            k_sc[at : at + 16, :] = ref[rel % 4, pair * 16 : (pair + 1) * 16, :]
            v_sc[at : at + 16, :] = ref[rel % 4, 64 + pair * 16 : 64 + (pair + 1) * 16, :]
    n = lax.broadcasted_iota(jnp.int32, (1, 1024), 1)
    rel = (n >> 4) & 15
    of = (((x - (rel >> 2)) & 3) << 2) + ((c ^ ((rel >> 1) & 1)) << 1) + (h ^ (rel & 1))
    col_block = (((n >> 8) * 2 + ((n >> 3) & 1)) << 4) + of
    kept = (col_block < gone) | (col_block >= back)
    for zz in range(RUN):
        wide = (zz // 2 + 1) * 256
        q = block_of(qg_ref, zz, 0)
        g = block_of(qg_ref, zz, 1)
        k = block_of(kv_ref, zz, 0)
        v = block_of(kv_ref, zz, 1)
        current = zz * 16 + residue
        alive = jnp.where((current < gone) | (current >= back), 1.0, 0.0)
        bias = jnp.where((col_block < current) & kept, 0.0, NEG)[:, :wide]
        ks = k_sc[0:wide, :]
        vs = v_sc[0:wide, :]
        t_far = dot_nt(q, ks) * LOG2 + bias
        t_own = jnp.where(causal, dot_nt(q, k) * LOG2, NEG)
        top = jnp.maximum(row_max(t_far), row_max(t_own))
        p_far = jnp.exp2(t_far - top)
        p_own = jnp.exp2(t_own - top)
        inv = alive / (row_sum(p_far) + row_sum(p_own))
        p_far = p_far * inv
        p_own = p_own * inv
        low_far = p_far.astype(BF16)
        low_own = p_own.astype(BF16)
        out = (dot_nn(low_far, vs) + dot_nn(low_own, v)).astype(BF16)
        delta = row_sum(g.astype(F32) * out.astype(F32))
        ds_far = (p_far * (dot_nt(g, vs) - delta) * SCALE).astype(BF16)
        ds_own = (p_own * (dot_nt(g, v) - delta) * SCALE).astype(BF16)
        dq = (dot_nn(ds_far, ks) + dot_nn(ds_own, k)).astype(BF16)
        oq_ref[4 * zz : 4 * zz + 4, 0:ROWS, :] = out.reshape(4, ROWS, HD)
        oq_ref[4 * zz : 4 * zz + 4, ROWS : 2 * ROWS, :] = dq.reshape(4, ROWS, HD)
        dkv_ref[0, zz] = dot_tn(ds_own, q)
        dkv_ref[1, zz] = dot_tn(low_own, g)
        p_sc[zz * BLK : (zz + 1) * BLK, 0:wide] = low_far
        d_sc[zz * BLK : (zz + 1) * BLK, 0:wide] = ds_far
    for pair in range(4):
        low = pair * 256
        count = 32 - 8 * pair
        q_all = qg_ref[8 * pair :, 0:ROWS, :].reshape(count * ROWS, HD)
        g_all = qg_ref[8 * pair :, ROWS : 2 * ROWS, :].reshape(count * ROWS, HD)
        dk = dot_tn(d_sc[low:, low : low + 256], q_all).astype(BF16)
        dv = dot_tn(p_sc[low:, low : low + 256], g_all).astype(BF16)
        for rel in range(16):
            ref = outs[rel // 4]
            ref[rel % 4, pair * 16 : (pair + 1) * 16, :] = dk[rel * 16 : (rel + 1) * 16, :]
            ref[rel % 4, 64 + pair * 16 : 64 + (pair + 1) * 16, :] = dv[
                rel * 16 : (rel + 1) * 16, :
            ]


def strided_head(meta_ref, pick_ref, kv_ref, qg_ref, oq_ref, dkv_ref):
    residue = meta_ref[1] * 4 + meta_ref[2] * 2 + meta_ref[3]
    gone, back = meta_ref[5], meta_ref[6]
    causal = lax.broadcasted_iota(jnp.int32, (BLK, BLK), 0) >= lax.broadcasted_iota(
        jnp.int32, (BLK, BLK), 1
    )

    def load(at, a):
        return kv_ref[pl.ds(4 * at, 4), a * ROWS : (a + 1) * ROWS, :].reshape(BLK, HD)

    def is_kept(block):
        return (block < gone) | (block >= back)

    for zz in range(RUN):
        block = zz * 16 + residue
        q = block_of(qg_ref, zz, 0)
        g = block_of(qg_ref, zz, 1)
        at = [zz]
        keys = [block_of(kv_ref, zz, 0)]
        values = [block_of(kv_ref, zz, 1)]
        scores = [jnp.where(causal, dot_nt(q, keys[0]) * LOG2, NEG)]
        for slot in range(2 if zz else 0):
            behind = zz - pick_ref[block, slot]
            clipped = jnp.clip(behind, 0, RUN - 1)
            usable = (behind >= 0) & is_kept(clipped * 16 + residue)
            at.append(clipped)
            keys.append(load(clipped, 0))
            values.append(load(clipped, 1))
            scores.append(dot_nt(q, keys[-1]) * LOG2 + jnp.where(usable, 0.0, NEG))
        top = row_max(scores[0])
        for s in scores[1:]:
            top = jnp.maximum(top, row_max(s))
        weights = [jnp.exp2(s - top) for s in scores]
        total = row_sum(weights[0])
        for w in weights[1:]:
            total = total + row_sum(w)
        inv = jnp.where(is_kept(block), 1.0, 0.0) / total
        weights = [w * inv for w in weights]
        low = [w.astype(BF16) for w in weights]
        out = dot_nn(low[0], values[0])
        for w, v in zip(low[1:], values[1:]):
            out = out + dot_nn(w, v)
        out = out.astype(BF16)
        delta = row_sum(g.astype(F32) * out.astype(F32))
        dq = jnp.zeros((BLK, HD), F32)
        for i, (w, k, v) in enumerate(zip(weights, keys, values)):
            ds = (w * (dot_nt(g, v) - delta) * SCALE).astype(BF16)
            dq = dq + dot_nn(ds, k)
            dk = dot_tn(ds, q)
            dv = dot_tn(low[i], g)
            if i == 0:
                dkv_ref[0, zz] = dk
                dkv_ref[1, zz] = dv
            else:
                dkv_ref[0, at[i]] += dk
                dkv_ref[1, at[i]] += dv
        oq_ref[4 * zz : 4 * zz + 4, 0:ROWS, :] = out.reshape(4, ROWS, HD)
        oq_ref[4 * zz : 4 * zz + 4, ROWS : 2 * ROWS, :] = dq.astype(BF16).reshape(4, ROWS, HD)


def attend_body(meta_ref, pick_ref, kv_ref, qg_ref, s0, s1, s2, s3, *rest):
    oq_ref, dkv_ref, r0, r1, r2, r3, k_sc, v_sc, p_sc, d_sc = rest
    outs = (r0, r1, r2, r3)
    is_fixed = meta_ref[4] < 2

    @pl.when(is_fixed)
    def _():
        fixed_head(
            meta_ref, kv_ref, qg_ref, (s0, s1, s2, s3), oq_ref, dkv_ref, outs, k_sc, v_sc, p_sc, d_sc
        )

    @pl.when(jnp.logical_not(is_fixed))
    def _():
        for ref in outs:
            ref[...] = jnp.zeros((4, 128, HD), BF16)
        strided_head(meta_ref, pick_ref, kv_ref, qg_ref, oq_ref, dkv_ref)


def attend(meta, pick, kv, qg, parts):
    outs = (shape(HEADS, 2 * ROWS, HD), shape(2, RUN, BLK, HD, dtype=F32)) + (
        shape(4, 128, HD),
    ) * 4
    scratch = [pltpu.VMEM((1024, HD), BF16)] * 2 + [pltpu.VMEM((1024, 1024), BF16)] * 2
    return call(attend_body, outs, [SMEM, SMEM] + [VMEM] * 6, scratch)(meta, pick, kv, qg, *parts)


def combine_body(meta_ref, cols_ref, dkv_ref, sum_ref, out_ref):
    residue = meta_ref[1] * 4 + meta_ref[2] * 2 + meta_ref[3]
    is_fixed = meta_ref[4] < 2
    row = lax.broadcasted_iota(jnp.int32, (16, HD), 0)
    for zz in range(RUN):
        for c in range(SUMMARY):
            at = jnp.where(is_fixed, cols_ref[zz * 16 + residue, c] - 16 * c, -1)
            for a in range(2):
                i = a * 64 + zz * SUMMARY + c
                extra = jnp.broadcast_to(sum_ref[i : i + 1, :], (16, HD))
                value = dkv_ref[a, zz, 16 * c : 16 * (c + 1), :] + jnp.where(row == at, extra, 0.0)
                base = a * ROWS + 16 * (c % 2)
                out_ref[4 * zz + c // 2, base : base + 16, :] = value.astype(BF16)


def combine(meta, cols, dkv, total):
    return call(combine_body, shape(HEADS, 2 * ROWS, HD), [SMEM, SMEM, VMEM, VMEM])(
        meta, cols, dkv, total
    )


def exchange(block):
    return lax.all_to_all(block, GROUP, split_axis=0, concat_axis=0, tiled=True)


def swap(block, axis):
    return lax.ppermute(block, axis, [(0, 1), (1, 0)])


def turn(block, distance):
    return lax.ppermute(block, "x", [(i, (i + distance) % 4) for i in range(4)])


def gather_summaries(own):
    both = jnp.stack([own, swap(own, "h")])
    chip = jnp.concatenate([both, swap(both, "c")])
    return [chip] + [turn(chip, d) for d in range(1, 4)]


def scatter_partials(parts):
    total = parts[0].astype(F32)
    for d in range(1, 4):
        total = total + turn(parts[d], -d).astype(F32)
    total = total[:2] + swap(total[2:].astype(BF16), "c").astype(F32)
    return total[0] + swap(total[1].astype(BF16), "h").astype(F32)


def shards(query, key_in, value, out_grad, block_keep, strided_pick, summary_cols):
    ids = jnp.arange(block_keep.shape[0], dtype=jnp.int32)
    removed = block_keep != 1
    gone = jnp.min(jnp.where(removed, ids, ids.shape[0]))
    back = jnp.max(jnp.where(removed, ids + 1, 0))
    where = [lax.axis_index(name).astype(jnp.int32) for name in AXES]
    meta = jnp.stack(where + [gone, back])
    kv = exchange(pack(key_in, value))
    send, kv = lax.optimization_barrier((pack(query, out_grad), kv))
    qg = exchange(send)
    parts = gather_summaries(summary(meta, summary_cols, kv))
    oq, dkv, *partials = attend(meta, strided_pick, kv, qg, parts)
    first = exchange(oq)
    total = scatter_partials(partials)
    back_kv = exchange(combine(meta, summary_cols, dkv, total))
    attended, grad_query = unpack(first)
    grad_key, grad_value = unpack(back_kv)
    return attended, grad_query, grad_key, grad_value


def solution(mesh):
    split = Mesh(np.asarray(mesh.devices).reshape(8, 4, 2, 2, 4), AXES)
    tokens = P(AXES, None)
    return jax.shard_map(
        shards,
        mesh=split,
        in_specs=(tokens, tokens, tokens, tokens, P(), P(), P()),
        out_specs=(tokens, tokens, tokens, tokens),
        check_vma=False,
    )
```

```python
import math

import jax
import jax.numpy as jnp
import numpy as np
from jax import lax
from jax.experimental import pallas as pl
from jax.experimental.pallas import tpu as pltpu
from jax.sharding import Mesh
from jax.sharding import PartitionSpec as P

HD = 128
BLK = 128
SUMMARY = 8
ROWS = 32
HEADS = 32
RUN = 8
SCALE = 1.0 / math.sqrt(HD)
LOG2 = SCALE * math.log2(math.e)
NEG = -1e30

AXES = ("z", "x", "c", "h", "q")
GROUP = ("z", "q")

F32 = jnp.float32
BF16 = jnp.bfloat16

VMEM = pl.BlockSpec(memory_space=pltpu.VMEM)
SMEM = pl.BlockSpec(memory_space=pltpu.SMEM)
PARAMS = pltpu.CompilerParams(vmem_limit_bytes=56 * 1024 * 1024)


def dot(a, b, dims):
    return lax.dot_general(a, b, (dims, ((), ())), preferred_element_type=F32)


def dot_nt(a, b):
    return dot(a, b, ((1,), (1,)))


def dot_nn(a, b):
    return dot(a, b, ((1,), (0,)))


def dot_tn(a, b):
    return dot(a, b, ((0,), (0,)))


def row_max(a):
    return jnp.max(a, axis=1, keepdims=True)


def row_sum(a):
    return jnp.sum(a, axis=1, keepdims=True)


def shape(*dims, dtype=BF16):
    return jax.ShapeDtypeStruct(dims, dtype)


def call(body, out_shape, specs, scratch=()):
    return pl.pallas_call(
        body,
        out_shape=out_shape,
        in_specs=specs,
        out_specs=jax.tree.map(lambda _: VMEM, out_shape),
        scratch_shapes=list(scratch),
        compiler_params=PARAMS,
    )


def coord(name):
    return lax.axis_index(name).astype(jnp.int32)


def my_residue():
    return coord("x") * 4 + coord("c") * 2 + coord("h")


def pack_body(*refs):
    out_ref = refs[-1]
    for i, ref in enumerate(refs[:-1]):
        for d in range(HEADS):
            out_ref[d, i * ROWS : (i + 1) * ROWS, :] = ref[:, d * HD : (d + 1) * HD]


def pack(*arrays):
    return call(pack_body, shape(HEADS, 4 * ROWS, HD), [VMEM] * 4)(*arrays)


def unpack_body(x_ref, *refs):
    for i, ref in enumerate(refs):
        for d in range(HEADS):
            ref[:, d * HD : (d + 1) * HD] = x_ref[d, i * ROWS : (i + 1) * ROWS, :]


def unpack(x):
    return call(unpack_body, (shape(ROWS, HEADS * HD),) * 4, [VMEM])(x)


Q, K, V, G = range(4)


def block_of(ref, zz, a):
    return ref[4 * zz : 4 * zz + 4, a * ROWS : (a + 1) * ROWS, :].reshape(BLK, HD)


def summary_body(cols_ref, k_ref, v_ref, out_ref):
    block = coord("z") * 16 + my_residue()
    quarter = coord("q")
    row = lax.broadcasted_iota(jnp.int32, (8, ROWS), 0)
    lane = lax.broadcasted_iota(jnp.int32, (8, ROWS), 1)
    first = cols_ref[2 * quarter, block] - ROWS * quarter
    second = cols_ref[2 * quarter + 1, block] - ROWS * quarter
    hit = lane == jnp.where((row & 1) == 0, first, second)
    of_keys = (row & 2) == 0
    pick_k = (hit & of_keys).astype(F32).astype(BF16)
    pick_v = (hit & jnp.logical_not(of_keys)).astype(F32).astype(BF16)
    rows = dot_nn(pick_k, k_ref[...]) + dot_nn(pick_v, v_ref[...])
    upper = lax.broadcasted_iota(jnp.int32, (8, HD), 0) < 4
    for d in range(0, HEADS, 4):
        two = []
        for e in (d, d + 2):
            one = rows[:, e * HD : (e + 1) * HD]
            other = rows[:, (e + 1) * HD : (e + 2) * HD]
            two.append(jnp.where(upper, one, other))
        out_ref[4 * d : 4 * d + 16, :] = jnp.concatenate(two).astype(BF16)


def summary(cols, k, v):
    return call(summary_body, shape(4 * HEADS, HD), [SMEM, VMEM, VMEM])(cols, k, v)


def fixed_head(run_ref, x_ref, parts, oq_ref, dkv_ref, outs, k_sc, v_sc, p_sc, d_sc):
    x, c, h = coord("x"), coord("c"), coord("h")
    gone, back = run_ref[0], run_ref[1]
    residue = my_residue()
    causal = lax.broadcasted_iota(jnp.int32, (BLK, BLK), 0) >= lax.broadcasted_iota(
        jnp.int32, (BLK, BLK), 1
    )
    m = lax.broadcasted_iota(jnp.int32, (BLK, BLK), 0)
    source = ((m & 63) >> 3) * 16 + ((m & 7) >> 1) * 4 + (m >> 6) * 2 + (m & 1)
    order = (source == lax.broadcasted_iota(jnp.int32, (BLK, BLK), 1)).astype(F32).astype(BF16)
    for rel in range(16):
        rows = dot_nn(order, parts[rel // 4][rel % 4]).astype(BF16)
        for pair in range(4):
            at = pair * 256 + rel * 16
            k_sc[at : at + 16, :] = rows[pair * 16 : (pair + 1) * 16, :]
            v_sc[at : at + 16, :] = rows[64 + pair * 16 : 64 + (pair + 1) * 16, :]
    n = lax.broadcasted_iota(jnp.int32, (1, 1024), 1)
    rel = (n >> 4) & 15
    of = (((x - (rel >> 2)) & 3) << 2) + ((c ^ ((rel >> 1) & 1)) << 1) + (h ^ (rel & 1))
    col_block = (((n >> 8) * 2 + ((n >> 3) & 1)) << 4) + of
    kept = (col_block < gone) | (col_block >= back)
    for zz in range(RUN):
        wide = (zz // 2 + 1) * 256
        q = block_of(x_ref, zz, Q)
        g = block_of(x_ref, zz, G)
        k = block_of(x_ref, zz, K)
        v = block_of(x_ref, zz, V)
        current = zz * 16 + residue
        alive = jnp.where((current < gone) | (current >= back), 1.0, 0.0)
        bias = jnp.where((col_block < current) & kept, 0.0, NEG)[:, :wide]
        ks = k_sc[0:wide, :]
        vs = v_sc[0:wide, :]
        t_far = dot_nt(q, ks) * LOG2 + bias
        t_own = jnp.where(causal, dot_nt(q, k) * LOG2, NEG)
        top = jnp.maximum(row_max(t_far), row_max(t_own))
        p_far = jnp.exp2(t_far - top)
        p_own = jnp.exp2(t_own - top)
        inv = alive / (row_sum(p_far) + row_sum(p_own))
        p_far = p_far * inv
        p_own = p_own * inv
        low_far = p_far.astype(BF16)
        low_own = p_own.astype(BF16)
        out = (dot_nn(low_far, vs) + dot_nn(low_own, v)).astype(BF16)
        delta = row_sum(g.astype(F32) * out.astype(F32))
        ds_far = (p_far * (dot_nt(g, vs) - delta) * SCALE).astype(BF16)
        ds_own = (p_own * (dot_nt(g, v) - delta) * SCALE).astype(BF16)
        dq = (dot_nn(ds_far, ks) + dot_nn(ds_own, k)).astype(BF16)
        oq_ref[4 * zz : 4 * zz + 4, 0:ROWS, :] = out.reshape(4, ROWS, HD)
        oq_ref[4 * zz : 4 * zz + 4, ROWS : 2 * ROWS, :] = dq.reshape(4, ROWS, HD)
        dkv_ref[0, zz] = dot_tn(ds_own, q)
        dkv_ref[1, zz] = dot_tn(low_own, g)
        p_sc[zz * BLK : (zz + 1) * BLK, 0:wide] = low_far
        d_sc[zz * BLK : (zz + 1) * BLK, 0:wide] = ds_far
    for pair in range(4):
        low = pair * 256
        count = 32 - 8 * pair
        q_all = x_ref[8 * pair :, Q * ROWS : (Q + 1) * ROWS, :].reshape(count * ROWS, HD)
        g_all = x_ref[8 * pair :, G * ROWS : (G + 1) * ROWS, :].reshape(count * ROWS, HD)
        dk = dot_tn(d_sc[low:, low : low + 256], q_all).astype(BF16)
        dv = dot_tn(p_sc[low:, low : low + 256], g_all).astype(BF16)
        for rel in range(16):
            ref = outs[(rel >> 1) & 1]
            owner = ((x - (rel >> 2)) & 3) * 2 + (h ^ (rel & 1))
            ref[owner, pair * 16 : (pair + 1) * 16, :] = dk[rel * 16 : (rel + 1) * 16, :]
            ref[owner, 64 + pair * 16 : 64 + (pair + 1) * 16, :] = dv[
                rel * 16 : (rel + 1) * 16, :
            ]


def strided_head(run_ref, pick_ref, x_ref, oq_ref, dkv_ref):
    residue = my_residue()
    gone, back = run_ref[0], run_ref[1]
    causal = lax.broadcasted_iota(jnp.int32, (BLK, BLK), 0) >= lax.broadcasted_iota(
        jnp.int32, (BLK, BLK), 1
    )

    def load(at, a):
        return x_ref[pl.ds(4 * at, 4), a * ROWS : (a + 1) * ROWS, :].reshape(BLK, HD)

    def is_kept(block):
        return (block < gone) | (block >= back)

    for zz in range(RUN):
        block = zz * 16 + residue
        q = block_of(x_ref, zz, Q)
        g = block_of(x_ref, zz, G)
        at = [zz]
        keys = [block_of(x_ref, zz, K)]
        values = [block_of(x_ref, zz, V)]
        scores = [jnp.where(causal, dot_nt(q, keys[0]) * LOG2, NEG)]
        for slot in range(2 if zz else 0):
            behind = zz - pick_ref[slot, block]
            clipped = jnp.clip(behind, 0, RUN - 1)
            usable = (behind >= 0) & is_kept(clipped * 16 + residue)
            at.append(clipped)
            keys.append(load(clipped, K))
            values.append(load(clipped, V))
            scores.append(dot_nt(q, keys[-1]) * LOG2 + jnp.where(usable, 0.0, NEG))
        top = row_max(scores[0])
        for s in scores[1:]:
            top = jnp.maximum(top, row_max(s))
        weights = [jnp.exp2(s - top) for s in scores]
        total = row_sum(weights[0])
        for w in weights[1:]:
            total = total + row_sum(w)
        inv = jnp.where(is_kept(block), 1.0, 0.0) / total
        weights = [w * inv for w in weights]
        low = [w.astype(BF16) for w in weights]
        out = dot_nn(low[0], values[0])
        for w, v in zip(low[1:], values[1:]):
            out = out + dot_nn(w, v)
        out = out.astype(BF16)
        delta = row_sum(g.astype(F32) * out.astype(F32))
        dq = jnp.zeros((BLK, HD), F32)
        for i, (w, k, v) in enumerate(zip(weights, keys, values)):
            ds = (w * (dot_nt(g, v) - delta) * SCALE).astype(BF16)
            dq = dq + dot_nn(ds, k)
            dk = dot_tn(ds, q)
            dv = dot_tn(low[i], g)
            if i == 0:
                dkv_ref[0, zz] = dk
                dkv_ref[1, zz] = dv
            else:
                dkv_ref[0, at[i]] += dk
                dkv_ref[1, at[i]] += dv
        oq_ref[4 * zz : 4 * zz + 4, 0:ROWS, :] = out.reshape(4, ROWS, HD)
        oq_ref[4 * zz : 4 * zz + 4, ROWS : 2 * ROWS, :] = dq.astype(BF16).reshape(4, ROWS, HD)


def attend_body(run_ref, pick_ref, x_ref, s0, s1, s2, s3, *rest):
    oq_ref, dkv_ref, mine_ref, other_ref, k_sc, v_sc, p_sc, d_sc = rest
    outs = (mine_ref, other_ref)
    is_fixed = coord("q") < 2

    @pl.when(is_fixed)
    def _():
        fixed_head(run_ref, x_ref, (s0, s1, s2, s3), oq_ref, dkv_ref, outs, k_sc, v_sc, p_sc, d_sc)

    @pl.when(jnp.logical_not(is_fixed))
    def _():
        for ref in outs:
            ref[...] = jnp.zeros((8, 128, HD), BF16)
        strided_head(run_ref, pick_ref, x_ref, oq_ref, dkv_ref)


def attend(run, pick, x, parts):
    outs = (
        shape(HEADS, 2 * ROWS, HD),
        shape(2, RUN, BLK, HD, dtype=F32),
        shape(8, 128, HD),
        shape(8, 128, HD),
    )
    scratch = [pltpu.VMEM((1024, HD), BF16)] * 2 + [pltpu.VMEM((1024, 1024), BF16)] * 2
    return call(attend_body, outs, [SMEM, SMEM] + [VMEM] * 5, scratch)(run, pick, x, *parts)


def combine_body(cols_ref, oq_ref, dkv_ref, sum_ref, out_ref):
    residue = my_residue()
    is_fixed = coord("q") < 2
    total = sum_ref[0].astype(F32)
    for i in range(1, 8):
        total = total + sum_ref[i].astype(F32)
    row = lax.broadcasted_iota(jnp.int32, (16, HD), 0)
    for zz in range(RUN):
        for c in range(SUMMARY):
            at = jnp.where(is_fixed, cols_ref[c, zz * 16 + residue] - 16 * c, -1)
            for a in range(2):
                i = a * 64 + zz * SUMMARY + c
                extra = jnp.broadcast_to(total[i : i + 1, :], (16, HD))
                value = dkv_ref[a, zz, 16 * c : 16 * (c + 1), :] + jnp.where(row == at, extra, 0.0)
                base = (2 + a) * ROWS + 16 * (c % 2)
                out_ref[4 * zz + c // 2, base : base + 16, :] = value.astype(BF16)
    for d in range(HEADS):
        out_ref[d, 0 : 2 * ROWS, :] = oq_ref[d]


def combine(cols, oq, dkv, sums):
    return call(combine_body, shape(HEADS, 4 * ROWS, HD), [SMEM] + [VMEM] * 3)(cols, oq, dkv, sums)


def exchange(block, axes):
    return lax.all_to_all(block, axes, split_axis=0, concat_axis=0, tiled=True)


def near(block, bits):
    return lax.ppermute(block, ("c", "h"), [(i, i ^ bits) for i in range(4)])


def turn(block, distance):
    return lax.ppermute(block, "x", [(i, (i + distance) % 4) for i in range(4)])


def gather_summaries(own):
    chips = jnp.stack([own] + [near(own, bits) for bits in range(1, 4)])
    return [chips] + [turn(chips, d) for d in range(1, 4)]


def scatter_partials(mine, other):
    total = mine.astype(F32) + near(other, 2).astype(F32)
    return exchange(total.astype(BF16), ("x", "h"))


def shards(query, key_in, value, out_grad, block_keep, strided_pick, summary_cols):
    cols = summary_cols.T
    ids = jnp.arange(block_keep.shape[0], dtype=jnp.int32)
    removed = block_keep != 1
    gone = jnp.min(jnp.where(removed, ids, ids.shape[0]))
    run = jnp.stack([gone, jnp.max(jnp.where(removed, ids + 1, 0))])
    own = exchange(summary(cols, key_in, value), GROUP)
    send, own = lax.optimization_barrier((pack(query, key_in, value, out_grad), own))
    got = exchange(send, GROUP)
    oq, dkv, mine, other = attend(run, strided_pick.T, got, gather_summaries(own))
    sums = scatter_partials(mine, other)
    return tuple(unpack(exchange(combine(cols, oq, dkv, sums), GROUP)))


def solution(mesh):
    split = Mesh(np.asarray(mesh.devices).reshape(8, 4, 2, 2, 4), AXES)
    tokens = P(AXES, None)
    return jax.shard_map(
        shards,
        mesh=split,
        in_specs=(tokens, tokens, tokens, tokens, P(), P(), P()),
        out_specs=(tokens, tokens, tokens, tokens),
        check_vma=False,
    )
```

```python
import math

import jax
import jax.numpy as jnp
import numpy as np
from jax import lax
from jax.experimental import pallas as pl
from jax.experimental.pallas import tpu as pltpu
from jax.sharding import Mesh
from jax.sharding import PartitionSpec as P

HD = 128
BLK = 128
CANDS = 4
ROWS = 32
HEADS = 32
RUN = 8
SCALE = 1.0 / math.sqrt(HD)
LOG2 = SCALE * math.log2(math.e)
NEG = -1e30

AXES = ("z", "x", "c", "h", "q")
GROUP = ("z", "q")
OWNERS = ("z", "x", "q")

F32 = jnp.float32
BF16 = jnp.bfloat16

VMEM = pl.BlockSpec(memory_space=pltpu.VMEM)
SMEM = pl.BlockSpec(memory_space=pltpu.SMEM)
PARAMS = pltpu.CompilerParams(vmem_limit_bytes=56 * 1024 * 1024)


def dot(a, b, dims):
    return lax.dot_general(a, b, (dims, ((), ())), preferred_element_type=F32)


def dot_nt(a, b):
    return dot(a, b, ((1,), (1,)))


def dot_nn(a, b):
    return dot(a, b, ((1,), (0,)))


def dot_tn(a, b):
    return dot(a, b, ((0,), (0,)))


def row_max(a):
    return jnp.max(a, axis=1, keepdims=True)


def row_sum(a):
    return jnp.sum(a, axis=1, keepdims=True)


def shape(*dims, dtype=BF16):
    return jax.ShapeDtypeStruct(dims, dtype)


def call(body, out_shape, specs, scratch=()):
    return pl.pallas_call(
        body,
        out_shape=out_shape,
        in_specs=specs,
        out_specs=jax.tree.map(lambda _: VMEM, out_shape),
        scratch_shapes=list(scratch),
        compiler_params=PARAMS,
    )


def coord(name):
    return lax.axis_index(name).astype(jnp.int32)


def my_residue():
    return coord("x") * 4 + coord("c") * 2 + coord("h")


def pack_body(*refs):
    out_ref = refs[-1]
    for i, ref in enumerate(refs[:-1]):
        for d in range(HEADS):
            out_ref[d, i * ROWS : (i + 1) * ROWS, :] = ref[:, d * HD : (d + 1) * HD]


def pack(*arrays):
    return call(pack_body, shape(HEADS, 4 * ROWS, HD), [VMEM] * 4)(*arrays)


def unpack_body(x_ref, *refs):
    for i, ref in enumerate(refs):
        for d in range(HEADS):
            ref[:, d * HD : (d + 1) * HD] = x_ref[d, i * ROWS : (i + 1) * ROWS, :]


def unpack(x):
    return call(unpack_body, (shape(ROWS, HEADS * HD),) * 2, [VMEM])(x)


Q, K, V, G = range(4)


def block_of(ref, zz, a):
    return ref[4 * zz : 4 * zz + 4, a * ROWS : (a + 1) * ROWS, :].reshape(BLK, HD)


def summary_body(cols_ref, k_ref, v_ref, out_ref):
    block = coord("z") * 16 + my_residue()
    quarter = coord("q")
    row = lax.broadcasted_iota(jnp.int32, (8, ROWS), 0)
    lane = lax.broadcasted_iota(jnp.int32, (8, ROWS), 1)
    first = cols_ref[2 * quarter, block] - ROWS * quarter
    second = cols_ref[2 * quarter + 1, block] - ROWS * quarter
    hit = lane == jnp.where((row & 1) == 0, first, second)
    of_keys = (row & 2) == 0
    pick_k = (hit & of_keys).astype(F32).astype(BF16)
    pick_v = (hit & jnp.logical_not(of_keys)).astype(F32).astype(BF16)
    rows = dot_nn(pick_k, k_ref[...]) + dot_nn(pick_v, v_ref[...])
    upper = lax.broadcasted_iota(jnp.int32, (8, HD), 0) < 4
    for d in range(0, HEADS, 4):
        two = []
        for e in (d, d + 2):
            one = rows[:, e * HD : (e + 1) * HD]
            other = rows[:, (e + 1) * HD : (e + 2) * HD]
            two.append(jnp.where(upper, one, other))
        four = jnp.concatenate(two).astype(BF16)
        for x in range(4):
            at = (d // 4) * 64 + x * 16
            out_ref[at : at + 16, :] = four


def summary(cols, k, v):
    return call(summary_body, shape(16 * HEADS, HD), [SMEM, VMEM, VMEM])(cols, k, v)


def causal_mask():
    rows = lax.broadcasted_iota(jnp.int32, (BLK, BLK), 0)
    return rows >= lax.broadcasted_iota(jnp.int32, (BLK, BLK), 1)


def is_kept(run_ref, block):
    return (block < run_ref[0]) | (block >= run_ref[1])


def attend_block(q, k, v, g, causal, alive, far):
    t_own = jnp.where(causal, dot_nt(q, k) * LOG2, NEG)
    top = row_max(t_own)
    if far:
        ks, vs, bias = far
        t_far = dot_nt(q, ks) * LOG2 + bias
        top = jnp.maximum(top, row_max(t_far))
        p_far = jnp.exp2(t_far - top)
    p_own = jnp.exp2(t_own - top)
    total = row_sum(p_own)
    if far:
        total = total + row_sum(p_far)
    inv = alive / total
    p_own = p_own * inv
    low_own = p_own.astype(BF16)
    out = dot_nn(low_own, v)
    if far:
        p_far = p_far * inv
        low_far = p_far.astype(BF16)
        out = out + dot_nn(low_far, vs)
    out = out.astype(BF16)
    delta = row_sum(g.astype(F32) * out.astype(F32))
    ds_own = (p_own * (dot_nt(g, v) - delta) * SCALE).astype(BF16)
    dq = dot_nn(ds_own, k)
    if not far:
        return out, dq.astype(BF16), ds_own, low_own, None, None
    ds_far = (p_far * (dot_nt(g, vs) - delta) * SCALE).astype(BF16)
    dq = dq + dot_nn(ds_far, ks)
    return out, dq.astype(BF16), ds_own, low_own, ds_far, low_far


def store(ref, zz, a, rows):
    ref[4 * zz : 4 * zz + 4, a * ROWS : (a + 1) * ROWS, :] = rows.astype(BF16).reshape(4, ROWS, HD)


def rows_of(ref, low, high, a):
    count = (high - low) * BLK
    return ref[4 * low : 4 * high, a * ROWS : (a + 1) * ROWS, :].reshape(count, HD)


def fixed_head(run_ref, x_ref, parts, outs, out_ref, k_sc, v_sc, p_sc, d_sc):
    c, h = coord("c"), coord("h")
    residue = my_residue()
    causal = causal_mask()
    m = lax.broadcasted_iota(jnp.int32, (BLK, BLK), 0)
    source = ((m & 63) >> 3) * 16 + ((m & 7) >> 1) * 4 + (m >> 6) * 2 + (m & 1)
    order = (source == lax.broadcasted_iota(jnp.int32, (BLK, BLK), 1)).astype(F32).astype(BF16)
    for rel in range(16):
        x, near_by = rel // 4, rel % 4
        mixed = jnp.concatenate(
            [parts[near_by][z * 64 + x * 16 : z * 64 + x * 16 + 16, :] for z in range(RUN)]
        )
        rows = dot_nn(order, mixed).astype(BF16)
        for pair in range(4):
            at = pair * 256 + rel * 16
            k_sc[at : at + 16, :] = rows[pair * 16 : (pair + 1) * 16, :]
            v_sc[at : at + 16, :] = rows[64 + pair * 16 : 64 + (pair + 1) * 16, :]
    n = lax.broadcasted_iota(jnp.int32, (1, 1024), 1)
    rel = (n >> 4) & 15
    of = ((rel >> 2) << 2) + ((c ^ ((rel >> 1) & 1)) << 1) + (h ^ (rel & 1))
    col_block = (((n >> 8) * 2 + ((n >> 3) & 1)) << 4) + of
    kept = is_kept(run_ref, col_block)
    for zz in range(RUN):
        wide = (zz // 2 + 1) * 256
        q, k, v, g = (block_of(x_ref, zz, a) for a in (Q, K, V, G))
        current = zz * 16 + residue
        alive = jnp.where(is_kept(run_ref, current), 1.0, 0.0)
        bias = jnp.where((col_block < current) & kept, 0.0, NEG)[:, :wide]
        far = (k_sc[0:wide, :], v_sc[0:wide, :], bias)
        out, dq, ds_own, low_own, ds_far, low_far = attend_block(q, k, v, g, causal, alive, far)
        store(out_ref, zz, 0, out)
        store(out_ref, zz, 1, dq)
        store(out_ref, zz, 2, dot_tn(ds_own, q))
        store(out_ref, zz, 3, dot_tn(low_own, g))
        p_sc[zz * BLK : (zz + 1) * BLK, 0:wide] = low_far
        d_sc[zz * BLK : (zz + 1) * BLK, 0:wide] = ds_far
    for pair in range(4):
        low = pair * 256
        dk = dot_tn(d_sc[low:, low : low + 256], rows_of(x_ref, 2 * pair, RUN, Q))
        dv = dot_tn(p_sc[low:, low : low + 256], rows_of(x_ref, 2 * pair, RUN, G))
        k_sc[low : low + 256, :] = dk.astype(BF16)
        v_sc[low : low + 256, :] = dv.astype(BF16)
    for rel in range(16):
        x, near_by = rel // 4, rel % 4
        rows = jnp.concatenate(
            [
                ref[pair * 256 + rel * 16 : pair * 256 + rel * 16 + 16, :]
                for ref in (k_sc, v_sc)
                for pair in range(4)
            ]
        )
        mixed = dot_tn(order, rows).astype(BF16)
        for z in range(RUN):
            outs[near_by][z * 64 + x * 16 : z * 64 + x * 16 + 16, :] = mixed[
                z * 16 : (z + 1) * 16, :
            ]


def strided_head(run_ref, pick_ref, x_ref, out_ref, sum_sc):
    residue = my_residue()
    causal = causal_mask()
    for zz in range(RUN):
        block = zz * 16 + residue
        count = min(zz, CANDS)
        q, k, v, g = (block_of(x_ref, zz, a) for a in (Q, K, V, G))
        alive = jnp.where(is_kept(run_ref, block), 1.0, 0.0)
        far = None
        if count:
            first = zz - count
            col = lax.broadcasted_iota(jnp.int32, (1, count * BLK), 1) >> 7
            bias = jnp.full((1, count * BLK), NEG, F32)
            for i in range(count):
                m = count - i
                picked = (pick_ref[0, block] == m) | (pick_ref[1, block] == m)
                usable = picked & is_kept(run_ref, block - 16 * m)
                bias = jnp.where(col == i, jnp.where(usable, 0.0, NEG), bias)
            far = (rows_of(x_ref, first, zz, K), rows_of(x_ref, first, zz, V), bias)
        out, dq, ds_own, low_own, ds_far, low_far = attend_block(q, k, v, g, causal, alive, far)
        store(out_ref, zz, 0, out)
        store(out_ref, zz, 1, dq)
        sum_sc[0, zz * BLK : (zz + 1) * BLK, :] = dot_tn(ds_own, q)
        sum_sc[1, zz * BLK : (zz + 1) * BLK, :] = dot_tn(low_own, g)
        if count:
            sum_sc[0, first * BLK : zz * BLK, :] += dot_tn(ds_far, q)
            sum_sc[1, first * BLK : zz * BLK, :] += dot_tn(low_far, g)
    for zz in range(RUN):
        for a in range(2):
            store(out_ref, zz, 2 + a, sum_sc[a, zz * BLK : (zz + 1) * BLK, :])


def attend_body(run_ref, pick_ref, x_ref, s0, s1, s2, s3, *rest):
    out_ref, r0, r1, r2, r3, k_sc, v_sc, p_sc, d_sc, sum_sc = rest
    outs = (r0, r1, r2, r3)
    is_fixed = coord("q") < 2

    @pl.when(is_fixed)
    def _():
        fixed_head(run_ref, x_ref, (s0, s1, s2, s3), outs, out_ref, k_sc, v_sc, p_sc, d_sc)

    @pl.when(jnp.logical_not(is_fixed))
    def _():
        for ref in outs:
            ref[...] = jnp.zeros((512, HD), BF16)
        strided_head(run_ref, pick_ref, x_ref, out_ref, sum_sc)


def attend(run, pick, x, parts):
    outs = (shape(HEADS, 4 * ROWS, HD),) + (shape(512, HD),) * 4
    scratch = (
        [pltpu.VMEM((1024, HD), BF16)] * 2
        + [pltpu.VMEM((1024, 1024), BF16)] * 2
        + [pltpu.VMEM((2, 1024, HD), F32)]
    )
    return call(attend_body, outs, [SMEM, SMEM] + [VMEM] * 5, scratch)(run, pick, x, *parts)


def finish_body(cols_ref, x_ref, sum_ref, dk_ref, dv_ref):
    block = coord("z") * 16 + my_residue()
    quarter = coord("q")
    row = lax.broadcasted_iota(jnp.int32, (16, HD), 0)
    at = [cols_ref[2 * quarter + i, block] - ROWS * quarter - 16 * i for i in range(2)]
    for d in range(HEADS):
        lanes = slice(d * HD, (d + 1) * HD)
        if d % 4 >= 2:
            for a, ref in enumerate((dk_ref, dv_ref)):
                ref[:, lanes] = x_ref[d, (2 + a) * ROWS : (3 + a) * ROWS, :]
            continue
        if d % 4 == 0:
            base = (d // 4) * 64
            total = sum_ref[base : base + 16, :].astype(F32)
            for x in range(1, 4):
                total = total + sum_ref[base + 16 * x : base + 16 * x + 16, :].astype(F32)
        for a, ref in enumerate((dk_ref, dv_ref)):
            for i in range(2):
                n = (d % 4) * 4 + a * 2 + i
                extra = jnp.broadcast_to(total[n : n + 1, :], (16, HD))
                low = (2 + a) * ROWS + 16 * i
                own = x_ref[d, low : low + 16, :].astype(F32)
                value = own + jnp.where(row == at[i], extra, 0.0)
                ref[16 * i : 16 * i + 16, lanes] = value.astype(BF16)


def finish(cols, x, sums):
    return call(finish_body, (shape(ROWS, HEADS * HD),) * 2, [SMEM, VMEM, VMEM])(cols, x, sums)


def exchange(block, axes):
    return lax.all_to_all(block, axes, split_axis=0, concat_axis=0, tiled=True)


def near(block, bits):
    return lax.ppermute(block, ("c", "h"), [(i, i ^ bits) for i in range(4)])


def scatter_partials(partials):
    total = partials[0].astype(F32)
    for bits in range(1, 4):
        total = total + near(partials[bits], bits).astype(F32)
    return exchange(total.astype(BF16), OWNERS)


def shards(query, key_in, value, out_grad, block_keep, strided_pick, summary_cols):
    cols = summary_cols.T
    ids = jnp.arange(block_keep.shape[0], dtype=jnp.int32)
    removed = block_keep != 1
    gone = jnp.min(jnp.where(removed, ids, ids.shape[0]))
    run = jnp.stack([gone, jnp.max(jnp.where(removed, ids + 1, 0))])
    own = exchange(summary(cols, key_in, value), OWNERS)
    send, own = lax.optimization_barrier((pack(query, key_in, value, out_grad), own))
    got = exchange(send, GROUP)
    parts = [own] + [near(own, bits) for bits in range(1, 4)]
    outs, *partials = attend(run, strided_pick.T, got, parts)
    back = exchange(outs, GROUP)
    sums = scatter_partials(partials)
    return tuple(unpack(back)) + tuple(finish(cols, back, sums))


def solution(mesh):
    split = Mesh(np.asarray(mesh.devices).reshape(8, 4, 2, 2, 4), AXES)
    tokens = P(AXES, None)
    return jax.shard_map(
        shards,
        mesh=split,
        in_specs=(tokens, tokens, tokens, tokens, P(), P(), P()),
        out_specs=(tokens, tokens, tokens, tokens),
        check_vma=False,
    )
```

```python
import math

import jax
import jax.numpy as jnp
import numpy as np
from jax import lax
from jax.experimental import pallas as pl
from jax.experimental.pallas import tpu as pltpu
from jax.sharding import Mesh
from jax.sharding import PartitionSpec as P

HD = 128
BLK = 128
CANDS = 4
ROWS = 32
HEADS = 32
RUN = 8
SCALE = 1.0 / math.sqrt(HD)
LOG2 = SCALE * math.log2(math.e)
NEG = -1e30

AXES = ("z", "x", "c", "h", "q")
GROUP = ("z", "q")
OWNERS = ("z", "h", "q")

F32 = jnp.float32
BF16 = jnp.bfloat16

VMEM = pl.BlockSpec(memory_space=pltpu.VMEM)
SMEM = pl.BlockSpec(memory_space=pltpu.SMEM)
PARAMS = pltpu.CompilerParams(vmem_limit_bytes=56 * 1024 * 1024)


def dot(a, b, dims):
    return lax.dot_general(a, b, (dims, ((), ())), preferred_element_type=F32)


def dot_nt(a, b):
    return dot(a, b, ((1,), (1,)))


def dot_nn(a, b):
    return dot(a, b, ((1,), (0,)))


def dot_tn(a, b):
    return dot(a, b, ((0,), (0,)))


def row_max(a):
    return jnp.max(a, axis=1, keepdims=True)


def row_sum(a):
    return jnp.sum(a, axis=1, keepdims=True)


def shape(*dims, dtype=BF16):
    return jax.ShapeDtypeStruct(dims, dtype)


def call(body, out_shape, specs, scratch=()):
    return pl.pallas_call(
        body,
        out_shape=out_shape,
        in_specs=specs,
        out_specs=jax.tree.map(lambda _: VMEM, out_shape),
        scratch_shapes=list(scratch),
        compiler_params=PARAMS,
    )


def coord(name):
    return lax.axis_index(name).astype(jnp.int32)


def my_residue():
    return coord("x") * 4 + coord("c") * 2 + coord("h")


def pack_body(*refs):
    out_ref = refs[-1]
    for i, ref in enumerate(refs[:-1]):
        for d in range(HEADS):
            out_ref[d, i * ROWS : (i + 1) * ROWS, :] = ref[:, d * HD : (d + 1) * HD]


def pack(*arrays):
    return call(pack_body, shape(HEADS, 4 * ROWS, HD), [VMEM] * 4)(*arrays)


def unpack_body(x_ref, *refs):
    for i, ref in enumerate(refs):
        for d in range(HEADS):
            ref[:, d * HD : (d + 1) * HD] = x_ref[d, i * ROWS : (i + 1) * ROWS, :]


def unpack(x):
    return call(unpack_body, (shape(ROWS, HEADS * HD),) * 2, [VMEM])(x)


Q, K, V, G = range(4)


def block_of(ref, zz, a):
    return ref[4 * zz : 4 * zz + 4, a * ROWS : (a + 1) * ROWS, :].reshape(BLK, HD)


def summary_body(cols_ref, k_ref, v_ref, out_ref):
    block = coord("z") * 16 + my_residue()
    quarter = coord("q")
    row = lax.broadcasted_iota(jnp.int32, (8, ROWS), 0)
    lane = lax.broadcasted_iota(jnp.int32, (8, ROWS), 1)
    first = cols_ref[2 * quarter, block] - ROWS * quarter
    second = cols_ref[2 * quarter + 1, block] - ROWS * quarter
    hit = lane == jnp.where((row & 1) == 0, first, second)
    of_keys = (row & 2) == 0
    pick_k = (hit & of_keys).astype(F32).astype(BF16)
    pick_v = (hit & jnp.logical_not(of_keys)).astype(F32).astype(BF16)
    rows = dot_nn(pick_k, k_ref[...]) + dot_nn(pick_v, v_ref[...])
    upper = lax.broadcasted_iota(jnp.int32, (8, HD), 0) < 4
    for d in range(0, HEADS, 4):
        two = []
        for e in (d, d + 2):
            one = rows[:, e * HD : (e + 1) * HD]
            other = rows[:, (e + 1) * HD : (e + 2) * HD]
            two.append(jnp.where(upper, one, other))
        four = jnp.concatenate(two).astype(BF16)
        for h in range(2):
            at = (d // 4) * 32 + h * 16
            out_ref[at : at + 16, :] = four


def summary(cols, k, v):
    return call(summary_body, shape(8 * HEADS, HD), [SMEM, VMEM, VMEM])(cols, k, v)


def causal_mask():
    rows = lax.broadcasted_iota(jnp.int32, (BLK, BLK), 0)
    return rows >= lax.broadcasted_iota(jnp.int32, (BLK, BLK), 1)


def is_kept(run_ref, block):
    return (block < run_ref[0]) | (block >= run_ref[1])


def attend_block(q, k, v, g, causal, alive, far):
    t_own = jnp.where(causal, dot_nt(q, k) * LOG2, NEG)
    top = row_max(t_own)
    if far:
        ks, vs, bias = far
        t_far = dot_nt(q, ks) * LOG2 + bias
        top = jnp.maximum(top, row_max(t_far))
        p_far = jnp.exp2(t_far - top)
    p_own = jnp.exp2(t_own - top)
    total = row_sum(p_own)
    if far:
        total = total + row_sum(p_far)
    inv = alive / total
    p_own = p_own * inv
    low_own = p_own.astype(BF16)
    out = dot_nn(low_own, v)
    if far:
        p_far = p_far * inv
        low_far = p_far.astype(BF16)
        out = out + dot_nn(low_far, vs)
    out = out.astype(BF16)
    delta = row_sum(g.astype(F32) * out.astype(F32))
    ds_own = (p_own * (dot_nt(g, v) - delta) * SCALE).astype(BF16)
    dq = dot_nn(ds_own, k)
    if not far:
        return out, dq.astype(BF16), ds_own, low_own, None, None
    ds_far = (p_far * (dot_nt(g, vs) - delta) * SCALE).astype(BF16)
    dq = dq + dot_nn(ds_far, ks)
    return out, dq.astype(BF16), ds_own, low_own, ds_far, low_far


def store(ref, zz, a, rows):
    ref[4 * zz : 4 * zz + 4, a * ROWS : (a + 1) * ROWS, :] = rows.astype(BF16).reshape(4, ROWS, HD)


def rows_of(ref, low, high, a):
    count = (high - low) * BLK
    return ref[4 * low : 4 * high, a * ROWS : (a + 1) * ROWS, :].reshape(count, HD)


def fixed_head(run_ref, x_ref, parts, outs, out_ref, k_sc, v_sc, p_sc, d_sc):
    x, c = coord("x"), coord("c")
    residue = my_residue()
    causal = causal_mask()
    m = lax.broadcasted_iota(jnp.int32, (BLK, BLK), 0)
    source = ((m & 63) >> 3) * 16 + ((m & 7) >> 1) * 4 + (m >> 6) * 2 + (m & 1)
    order = (source == lax.broadcasted_iota(jnp.int32, (BLK, BLK), 1)).astype(F32).astype(BF16)
    for rel in range(16):
        base = ((rel >> 1) & 1) * 256 + (rel & 1) * 16
        mixed = jnp.concatenate(
            [parts[rel // 4][base + z * 32 : base + z * 32 + 16, :] for z in range(RUN)]
        )
        rows = dot_nn(order, mixed).astype(BF16)
        for pair in range(4):
            at = pair * 256 + rel * 16
            k_sc[at : at + 16, :] = rows[pair * 16 : (pair + 1) * 16, :]
            v_sc[at : at + 16, :] = rows[64 + pair * 16 : 64 + (pair + 1) * 16, :]
    n = lax.broadcasted_iota(jnp.int32, (1, 1024), 1)
    rel = (n >> 4) & 15
    of = (((x - (rel >> 2)) & 3) << 2) + ((c ^ ((rel >> 1) & 1)) << 1) + (rel & 1)
    col_block = (((n >> 8) * 2 + ((n >> 3) & 1)) << 4) + of
    kept = is_kept(run_ref, col_block)
    for zz in range(RUN):
        wide = (zz // 2 + 1) * 256
        q, k, v, g = (block_of(x_ref, zz, a) for a in (Q, K, V, G))
        current = zz * 16 + residue
        alive = jnp.where(is_kept(run_ref, current), 1.0, 0.0)
        bias = jnp.where((col_block < current) & kept, 0.0, NEG)[:, :wide]
        far = (k_sc[0:wide, :], v_sc[0:wide, :], bias)
        out, dq, ds_own, low_own, ds_far, low_far = attend_block(q, k, v, g, causal, alive, far)
        store(out_ref, zz, 0, out)
        store(out_ref, zz, 1, dq)
        store(out_ref, zz, 2, dot_tn(ds_own, q))
        store(out_ref, zz, 3, dot_tn(low_own, g))
        p_sc[zz * BLK : (zz + 1) * BLK, 0:wide] = low_far
        d_sc[zz * BLK : (zz + 1) * BLK, 0:wide] = ds_far
    for pair in range(4):
        low = pair * 256
        dk = dot_tn(d_sc[low:, low : low + 256], rows_of(x_ref, 2 * pair, RUN, Q))
        dv = dot_tn(p_sc[low:, low : low + 256], rows_of(x_ref, 2 * pair, RUN, G))
        k_sc[low : low + 256, :] = dk.astype(BF16)
        v_sc[low : low + 256, :] = dv.astype(BF16)
    for rel in range(16):
        base = ((rel >> 1) & 1) * 256 + (rel & 1) * 16
        rows = jnp.concatenate(
            [
                ref[pair * 256 + rel * 16 : pair * 256 + rel * 16 + 16, :]
                for ref in (k_sc, v_sc)
                for pair in range(4)
            ]
        )
        mixed = dot_tn(order, rows).astype(BF16)
        for z in range(RUN):
            outs[rel // 4][base + z * 32 : base + z * 32 + 16, :] = mixed[z * 16 : (z + 1) * 16, :]


def strided_head(run_ref, pick_ref, x_ref, out_ref, sum_sc):
    residue = my_residue()
    causal = causal_mask()
    for zz in range(RUN):
        block = zz * 16 + residue
        count = min(zz, CANDS)
        q, k, v, g = (block_of(x_ref, zz, a) for a in (Q, K, V, G))
        alive = jnp.where(is_kept(run_ref, block), 1.0, 0.0)
        far = None
        if count:
            first = zz - count
            col = lax.broadcasted_iota(jnp.int32, (1, count * BLK), 1) >> 7
            bias = jnp.full((1, count * BLK), NEG, F32)
            for i in range(count):
                m = count - i
                picked = (pick_ref[0, block] == m) | (pick_ref[1, block] == m)
                usable = picked & is_kept(run_ref, block - 16 * m)
                bias = jnp.where(col == i, jnp.where(usable, 0.0, NEG), bias)
            far = (rows_of(x_ref, first, zz, K), rows_of(x_ref, first, zz, V), bias)
        out, dq, ds_own, low_own, ds_far, low_far = attend_block(q, k, v, g, causal, alive, far)
        store(out_ref, zz, 0, out)
        store(out_ref, zz, 1, dq)
        sum_sc[0, zz * BLK : (zz + 1) * BLK, :] = dot_tn(ds_own, q)
        sum_sc[1, zz * BLK : (zz + 1) * BLK, :] = dot_tn(low_own, g)
        if count:
            sum_sc[0, first * BLK : zz * BLK, :] += dot_tn(ds_far, q)
            sum_sc[1, first * BLK : zz * BLK, :] += dot_tn(low_far, g)
    for zz in range(RUN):
        for a in range(2):
            store(out_ref, zz, 2 + a, sum_sc[a, zz * BLK : (zz + 1) * BLK, :])


def attend_body(run_ref, pick_ref, x_ref, s0, s1, s2, s3, *rest):
    out_ref, r0, r1, r2, r3, k_sc, v_sc, p_sc, d_sc, sum_sc = rest
    outs = (r0, r1, r2, r3)
    is_fixed = coord("q") < 2

    @pl.when(is_fixed)
    def _():
        fixed_head(run_ref, x_ref, (s0, s1, s2, s3), outs, out_ref, k_sc, v_sc, p_sc, d_sc)

    @pl.when(jnp.logical_not(is_fixed))
    def _():
        for ref in outs:
            ref[...] = jnp.zeros((512, HD), BF16)
        strided_head(run_ref, pick_ref, x_ref, out_ref, sum_sc)


def attend(run, pick, x, parts):
    outs = (shape(HEADS, 4 * ROWS, HD),) + (shape(512, HD),) * 4
    scratch = (
        [pltpu.VMEM((1024, HD), BF16)] * 2
        + [pltpu.VMEM((1024, 1024), BF16)] * 2
        + [pltpu.VMEM((2, 1024, HD), F32)]
    )
    return call(attend_body, outs, [SMEM, SMEM] + [VMEM] * 5, scratch)(run, pick, x, *parts)


def finish_body(cols_ref, x_ref, sum_ref, dk_ref, dv_ref):
    block = coord("z") * 16 + my_residue()
    quarter = coord("q")
    row = lax.broadcasted_iota(jnp.int32, (16, HD), 0)
    at = [cols_ref[2 * quarter + i, block] - ROWS * quarter - 16 * i for i in range(2)]
    for d in range(HEADS):
        lanes = slice(d * HD, (d + 1) * HD)
        if d % 4 >= 2:
            for a, ref in enumerate((dk_ref, dv_ref)):
                ref[:, lanes] = x_ref[d, (2 + a) * ROWS : (3 + a) * ROWS, :]
            continue
        if d % 4 == 0:
            base = (d // 4) * 32
            total = sum_ref[base : base + 16, :].astype(F32)
            total = total + sum_ref[base + 16 : base + 32, :].astype(F32)
        for a, ref in enumerate((dk_ref, dv_ref)):
            for i in range(2):
                n = (d % 4) * 4 + a * 2 + i
                extra = jnp.broadcast_to(total[n : n + 1, :], (16, HD))
                low = (2 + a) * ROWS + 16 * i
                own = x_ref[d, low : low + 16, :].astype(F32)
                value = own + jnp.where(row == at[i], extra, 0.0)
                ref[16 * i : 16 * i + 16, lanes] = value.astype(BF16)


def finish(cols, x, sums):
    return call(finish_body, (shape(ROWS, HEADS * HD),) * 2, [SMEM, VMEM, VMEM])(cols, x, sums)


def exchange(block, axes):
    return lax.all_to_all(block, axes, split_axis=0, concat_axis=0, tiled=True)


def swap(block):
    return lax.ppermute(block, "c", [(0, 1), (1, 0)])


def turn(block, distance):
    return lax.ppermute(block, "x", [(i, (i + distance) % 4) for i in range(4)])


def gather_summaries(own):
    chip = jnp.concatenate([own, swap(own)])
    return [chip] + [turn(chip, d) for d in range(1, 4)]


def scatter_partials(partials):
    total = partials[0].astype(F32)
    for d in range(1, 4):
        total = total + turn(partials[d], -d).astype(F32)
    half = total.shape[0] // 2
    total = total[:half] + swap(total[half:].astype(BF16)).astype(F32)
    return exchange(total.astype(BF16), OWNERS)


def shards(query, key_in, value, out_grad, block_keep, strided_pick, summary_cols):
    cols = summary_cols.T
    ids = jnp.arange(block_keep.shape[0], dtype=jnp.int32)
    removed = block_keep != 1
    gone = jnp.min(jnp.where(removed, ids, ids.shape[0]))
    run = jnp.stack([gone, jnp.max(jnp.where(removed, ids + 1, 0))])
    own = exchange(summary(cols, key_in, value), OWNERS)
    send, own = lax.optimization_barrier((pack(query, key_in, value, out_grad), own))
    got = exchange(send, GROUP)
    outs, *partials = attend(run, strided_pick.T, got, gather_summaries(own))
    back = exchange(outs, GROUP)
    sums = scatter_partials(partials)
    return tuple(unpack(back)) + tuple(finish(cols, back, sums))


def solution(mesh):
    split = Mesh(np.asarray(mesh.devices).reshape(8, 4, 2, 2, 4), AXES)
    tokens = P(AXES, None)
    return jax.shard_map(
        shards,
        mesh=split,
        in_specs=(tokens, tokens, tokens, tokens, P(), P(), P()),
        out_specs=(tokens, tokens, tokens, tokens),
        check_vma=False,
    )
```

```python
import math

import jax
import jax.numpy as jnp
import numpy as np
from jax import lax
from jax.experimental import pallas as pl
from jax.experimental.pallas import tpu as pltpu
from jax.sharding import Mesh
from jax.sharding import PartitionSpec as P

HD = 128
BLK = 128
CANDS = 4
ROWS = 32
HEADS = 32
RUN = 8
SCALE = 1.0 / math.sqrt(HD)
LOG2 = SCALE * math.log2(math.e)
NEG = -1e30

AXES = ("z", "x", "c", "h", "q")
GROUP = ("z", "q")
OWNERS = ("z", "h", "q")

F32 = jnp.float32
BF16 = jnp.bfloat16

VMEM = pl.BlockSpec(memory_space=pltpu.VMEM)
SMEM = pl.BlockSpec(memory_space=pltpu.SMEM)
PARAMS = pltpu.CompilerParams(vmem_limit_bytes=56 * 1024 * 1024)


def dot(a, b, dims):
    return lax.dot_general(a, b, (dims, ((), ())), preferred_element_type=F32)


def dot_nt(a, b):
    return dot(a, b, ((1,), (1,)))


def dot_nn(a, b):
    return dot(a, b, ((1,), (0,)))


def dot_tn(a, b):
    return dot(a, b, ((0,), (0,)))


def row_max(a):
    return jnp.max(a, axis=1, keepdims=True)


def row_sum(a):
    return jnp.sum(a, axis=1, keepdims=True)


def shape(*dims, dtype=BF16):
    return jax.ShapeDtypeStruct(dims, dtype)


def call(body, out_shape, specs, scratch=()):
    return pl.pallas_call(
        body,
        out_shape=out_shape,
        in_specs=specs,
        out_specs=jax.tree.map(lambda _: VMEM, out_shape),
        scratch_shapes=list(scratch),
        compiler_params=PARAMS,
    )


def coord(name):
    return lax.axis_index(name).astype(jnp.int32)


def my_residue():
    return coord("x") * 4 + coord("c") * 2 + coord("h")


def pack_body(*refs):
    out_ref = refs[-1]
    for i, ref in enumerate(refs[:-1]):
        for d in range(HEADS):
            out_ref[d, i * ROWS : (i + 1) * ROWS, :] = ref[:, d * HD : (d + 1) * HD]


def pack(*arrays):
    return call(pack_body, shape(HEADS, 4 * ROWS, HD), [VMEM] * 4)(*arrays)


def unpack_body(x_ref, *refs):
    for i, ref in enumerate(refs):
        for d in range(HEADS):
            ref[:, d * HD : (d + 1) * HD] = x_ref[d, i * ROWS : (i + 1) * ROWS, :]


def unpack(x):
    return call(unpack_body, (shape(ROWS, HEADS * HD),) * 2, [VMEM])(x)


Q, K, V, G = range(4)


def block_of(ref, zz, a):
    return ref[4 * zz : 4 * zz + 4, a * ROWS : (a + 1) * ROWS, :].reshape(BLK, HD)


def summary_body(cols_ref, k_ref, v_ref, out_ref):
    block = coord("z") * 16 + my_residue()
    quarter = coord("q")
    row = lax.broadcasted_iota(jnp.int32, (8, ROWS), 0)
    lane = lax.broadcasted_iota(jnp.int32, (8, ROWS), 1)
    first = cols_ref[2 * quarter, block] - ROWS * quarter
    second = cols_ref[2 * quarter + 1, block] - ROWS * quarter
    hit = lane == jnp.where((row & 1) == 0, first, second)
    of_keys = (row & 2) == 0
    pick_k = (hit & of_keys).astype(F32).astype(BF16)
    pick_v = (hit & jnp.logical_not(of_keys)).astype(F32).astype(BF16)
    rows = dot_nn(pick_k, k_ref[...]) + dot_nn(pick_v, v_ref[...])
    upper = lax.broadcasted_iota(jnp.int32, (8, HD), 0) < 4
    for d in range(0, HEADS, 4):
        two = []
        for e in (d, d + 2):
            one = rows[:, e * HD : (e + 1) * HD]
            other = rows[:, (e + 1) * HD : (e + 2) * HD]
            two.append(jnp.where(upper, one, other))
        four = jnp.concatenate(two).astype(BF16)
        for h in range(2):
            at = (d // 4) * 32 + h * 16
            out_ref[at : at + 16, :] = four


def summary(cols, k, v):
    return call(summary_body, shape(8 * HEADS, HD), [SMEM, VMEM, VMEM])(cols, k, v)


def causal_mask():
    rows = lax.broadcasted_iota(jnp.int32, (BLK, BLK), 0)
    return rows >= lax.broadcasted_iota(jnp.int32, (BLK, BLK), 1)


def is_kept(run_ref, block):
    return (block < run_ref[0]) | (block >= run_ref[1])


def attend_block(q, k, v, g, causal, alive, far):
    t_own = jnp.where(causal, dot_nt(q, k) * LOG2, NEG)
    top = row_max(t_own)
    if far:
        ks, vs, bias = far
        t_far = dot_nt(q, ks) * LOG2 + bias
        top = jnp.maximum(top, row_max(t_far))
        p_far = jnp.exp2(t_far - top)
    p_own = jnp.exp2(t_own - top)
    total = row_sum(p_own)
    if far:
        total = total + row_sum(p_far)
    inv = alive / total
    p_own = p_own * inv
    low_own = p_own.astype(BF16)
    out = dot_nn(low_own, v)
    if far:
        p_far = p_far * inv
        low_far = p_far.astype(BF16)
        out = out + dot_nn(low_far, vs)
    out = out.astype(BF16)
    delta = row_sum(g.astype(F32) * out.astype(F32))
    ds_own = (p_own * (dot_nt(g, v) - delta) * SCALE).astype(BF16)
    dq = dot_nn(ds_own, k)
    if not far:
        return out, dq.astype(BF16), ds_own, low_own, None, None
    ds_far = (p_far * (dot_nt(g, vs) - delta) * SCALE).astype(BF16)
    dq = dq + dot_nn(ds_far, ks)
    return out, dq.astype(BF16), ds_own, low_own, ds_far, low_far


def store(ref, zz, a, rows):
    ref[4 * zz : 4 * zz + 4, a * ROWS : (a + 1) * ROWS, :] = rows.astype(BF16).reshape(4, ROWS, HD)


def rows_of(ref, low, high, a):
    count = (high - low) * BLK
    return ref[4 * low : 4 * high, a * ROWS : (a + 1) * ROWS, :].reshape(count, HD)


def fixed_head(run_ref, x_ref, parts, outs, out_ref, k_sc, v_sc, p_sc, d_sc):
    x, c = coord("x"), coord("c")
    residue = my_residue()
    causal = causal_mask()
    m = lax.broadcasted_iota(jnp.int32, (BLK, BLK), 0)
    source = ((m & 63) >> 3) * 16 + ((m & 7) >> 1) * 4 + (m >> 6) * 2 + (m & 1)
    order = (source == lax.broadcasted_iota(jnp.int32, (BLK, BLK), 1)).astype(F32).astype(BF16)
    for rel in range(16):
        base = ((rel >> 1) & 1) * 256 + (rel & 1) * 16
        mixed = jnp.concatenate(
            [parts[rel // 4][base + z * 32 : base + z * 32 + 16, :] for z in range(RUN)]
        )
        rows = dot_nn(order, mixed).astype(BF16)
        for pair in range(4):
            at = pair * 256 + rel * 16
            k_sc[at : at + 16, :] = rows[pair * 16 : (pair + 1) * 16, :]
            v_sc[at : at + 16, :] = rows[64 + pair * 16 : 64 + (pair + 1) * 16, :]
    n = lax.broadcasted_iota(jnp.int32, (1, 1024), 1)
    rel = (n >> 4) & 15
    of = (((x - (rel >> 2)) & 3) << 2) + ((c ^ ((rel >> 1) & 1)) << 1) + (rel & 1)
    col_block = (((n >> 8) * 2 + ((n >> 3) & 1)) << 4) + of
    kept = is_kept(run_ref, col_block)
    for zz in range(RUN):
        wide = (zz // 2 + 1) * 256
        q, k, v, g = (block_of(x_ref, zz, a) for a in (Q, K, V, G))
        current = zz * 16 + residue
        alive = jnp.where(is_kept(run_ref, current), 1.0, 0.0)
        bias = jnp.where((col_block < current) & kept, 0.0, NEG)[:, :wide]
        far = (k_sc[0:wide, :], v_sc[0:wide, :], bias)
        out, dq, ds_own, low_own, ds_far, low_far = attend_block(q, k, v, g, causal, alive, far)
        store(out_ref, zz, 0, out)
        store(out_ref, zz, 1, dq)
        store(out_ref, zz, 2, dot_tn(ds_own, q))
        store(out_ref, zz, 3, dot_tn(low_own, g))
        p_sc[zz * BLK : (zz + 1) * BLK, 0:wide] = low_far
        d_sc[zz * BLK : (zz + 1) * BLK, 0:wide] = ds_far
    for pair in range(4):
        low = pair * 256
        dk = dot_tn(d_sc[low:, low : low + 256], rows_of(x_ref, 2 * pair, RUN, Q))
        dv = dot_tn(p_sc[low:, low : low + 256], rows_of(x_ref, 2 * pair, RUN, G))
        k_sc[low : low + 256, :] = dk.astype(BF16)
        v_sc[low : low + 256, :] = dv.astype(BF16)
    for rel in range(16):
        base = ((rel >> 1) & 1) * 256 + (rel & 1) * 16
        rows = jnp.concatenate(
            [
                ref[pair * 256 + rel * 16 : pair * 256 + rel * 16 + 16, :]
                for ref in (k_sc, v_sc)
                for pair in range(4)
            ]
        )
        mixed = dot_tn(order, rows).astype(BF16)
        for z in range(RUN):
            outs[rel // 4][base + z * 32 : base + z * 32 + 16, :] = mixed[z * 16 : (z + 1) * 16, :]


def strided_head(run_ref, pick_ref, x_ref, out_ref, sum_sc):
    residue = my_residue()
    causal = causal_mask()
    for zz in range(RUN):
        block = zz * 16 + residue
        count = min(zz, CANDS)
        q, k, v, g = (block_of(x_ref, zz, a) for a in (Q, K, V, G))
        alive = jnp.where(is_kept(run_ref, block), 1.0, 0.0)
        far = None
        if count:
            first = zz - count
            col = lax.broadcasted_iota(jnp.int32, (1, count * BLK), 1) >> 7
            bias = jnp.full((1, count * BLK), NEG, F32)
            for i in range(count):
                m = count - i
                picked = (pick_ref[0, block] == m) | (pick_ref[1, block] == m)
                usable = picked & is_kept(run_ref, block - 16 * m)
                bias = jnp.where(col == i, jnp.where(usable, 0.0, NEG), bias)
            far = (rows_of(x_ref, first, zz, K), rows_of(x_ref, first, zz, V), bias)
        out, dq, ds_own, low_own, ds_far, low_far = attend_block(q, k, v, g, causal, alive, far)
        store(out_ref, zz, 0, out)
        store(out_ref, zz, 1, dq)
        sum_sc[0, zz * BLK : (zz + 1) * BLK, :] = dot_tn(ds_own, q)
        sum_sc[1, zz * BLK : (zz + 1) * BLK, :] = dot_tn(low_own, g)
        if count:
            sum_sc[0, first * BLK : zz * BLK, :] += dot_tn(ds_far, q)
            sum_sc[1, first * BLK : zz * BLK, :] += dot_tn(low_far, g)
    for zz in range(RUN):
        for a in range(2):
            store(out_ref, zz, 2 + a, sum_sc[a, zz * BLK : (zz + 1) * BLK, :])


def attend_body(run_ref, pick_ref, x_ref, s0, s1, s2, s3, *rest):
    out_ref, r0, r1, r2, r3, k_sc, v_sc, p_sc, d_sc, sum_sc = rest
    outs = (r0, r1, r2, r3)
    is_fixed = coord("q") < 2

    @pl.when(is_fixed)
    def _():
        fixed_head(run_ref, x_ref, (s0, s1, s2, s3), outs, out_ref, k_sc, v_sc, p_sc, d_sc)

    @pl.when(jnp.logical_not(is_fixed))
    def _():
        for ref in outs:
            ref[...] = jnp.zeros((512, HD), BF16)
        strided_head(run_ref, pick_ref, x_ref, out_ref, sum_sc)


def attend(run, pick, x, parts):
    outs = (shape(HEADS, 4 * ROWS, HD),) + (shape(512, HD),) * 4
    scratch = (
        [pltpu.VMEM((1024, HD), BF16)] * 2
        + [pltpu.VMEM((1024, 1024), BF16)] * 2
        + [pltpu.VMEM((2, 1024, HD), F32)]
    )
    return call(attend_body, outs, [SMEM, SMEM] + [VMEM] * 5, scratch)(run, pick, x, *parts)


def finish_body(cols_ref, x_ref, sum_ref, dk_ref, dv_ref):
    block = coord("z") * 16 + my_residue()
    quarter = coord("q")
    row = lax.broadcasted_iota(jnp.int32, (16, HD), 0)
    at = [cols_ref[2 * quarter + i, block] - ROWS * quarter - 16 * i for i in range(2)]
    for d in range(HEADS):
        lanes = slice(d * HD, (d + 1) * HD)
        if d % 4 >= 2:
            for a, ref in enumerate((dk_ref, dv_ref)):
                ref[:, lanes] = x_ref[d, (2 + a) * ROWS : (3 + a) * ROWS, :]
            continue
        if d % 4 == 0:
            base = (d // 4) * 32
            total = sum_ref[base : base + 16, :].astype(F32)
            total = total + sum_ref[base + 16 : base + 32, :].astype(F32)
        for a, ref in enumerate((dk_ref, dv_ref)):
            for i in range(2):
                n = (d % 4) * 4 + a * 2 + i
                extra = jnp.broadcast_to(total[n : n + 1, :], (16, HD))
                low = (2 + a) * ROWS + 16 * i
                own = x_ref[d, low : low + 16, :].astype(F32)
                value = own + jnp.where(row == at[i], extra, 0.0)
                ref[16 * i : 16 * i + 16, lanes] = value.astype(BF16)


def finish(cols, x, sums):
    return call(finish_body, (shape(ROWS, HEADS * HD),) * 2, [SMEM, VMEM, VMEM])(cols, x, sums)


def here(block):
    return pltpu.with_memory_space_constraint(block, pltpu.VMEM)


def exchange(block, axes):
    return lax.all_to_all(block, axes, split_axis=0, concat_axis=0, tiled=True)


def swap(block):
    return lax.ppermute(block, "c", [(0, 1), (1, 0)])


def turn(block, distance):
    return lax.ppermute(block, "x", [(i, (i + distance) % 4) for i in range(4)])


def gather_summaries(own):
    chip = jnp.concatenate([own, swap(own)])
    return [chip] + [turn(chip, d) for d in range(1, 4)]


def scatter_partials(partials):
    total = partials[0].astype(F32)
    for d in range(1, 4):
        total = total + turn(partials[d], -d).astype(F32)
    half = total.shape[0] // 2
    total = total[:half] + swap(total[half:].astype(BF16)).astype(F32)
    return exchange(total.astype(BF16), OWNERS)


def shards(query, key_in, value, out_grad, block_keep, strided_pick, summary_cols):
    cols = summary_cols.T
    ids = jnp.arange(block_keep.shape[0], dtype=jnp.int32)
    removed = block_keep != 1
    gone = jnp.min(jnp.where(removed, ids, ids.shape[0]))
    run = jnp.stack([gone, jnp.max(jnp.where(removed, ids + 1, 0))])
    own = exchange(summary(cols, key_in, value), OWNERS)
    send, own = lax.optimization_barrier((pack(query, key_in, value, out_grad), own))
    got = exchange(send, GROUP)
    parts = [here(part) for part in gather_summaries(own)]
    outs, *partials = attend(run, strided_pick.T, here(got), parts)
    back = exchange(outs, GROUP)
    sums = scatter_partials(partials)
    back = here(back)
    return tuple(unpack(back)) + tuple(finish(cols, back, here(sums)))


def solution(mesh):
    split = Mesh(np.asarray(mesh.devices).reshape(8, 4, 2, 2, 4), AXES)
    tokens = P(AXES, None)
    return jax.shard_map(
        shards,
        mesh=split,
        in_specs=(tokens, tokens, tokens, tokens, P(), P(), P()),
        out_specs=(tokens, tokens, tokens, tokens),
        check_vma=False,
    )
```

```python
import math

import jax
import jax.numpy as jnp
import numpy as np
from jax import lax
from jax.experimental import pallas as pl
from jax.experimental.pallas import tpu as pltpu
from jax.sharding import Mesh
from jax.sharding import PartitionSpec as P

HD = 128
BLK = 128
CANDS = 4
ROWS = 32
HEADS = 32
RUN = 8
SIDE = 8
SCALE = 1.0 / math.sqrt(HD)
LOG2 = SCALE * math.log2(math.e)
NEG = -1e30

AXES = ("z", "x", "c", "h", "q")
GROUP = ("z", "q")
OWNERS = ("z", "h", "q")

F32 = jnp.float32
BF16 = jnp.bfloat16

VMEM = pl.BlockSpec(memory_space=pltpu.VMEM)
SMEM = pl.BlockSpec(memory_space=pltpu.SMEM)
PARAMS = pltpu.CompilerParams(vmem_limit_bytes=56 * 1024 * 1024)


def dot(a, b, dims):
    return lax.dot_general(a, b, (dims, ((), ())), preferred_element_type=F32)


def dot_nt(a, b):
    return dot(a, b, ((1,), (1,)))


def dot_nn(a, b):
    return dot(a, b, ((1,), (0,)))


def dot_tn(a, b):
    return dot(a, b, ((0,), (0,)))


def row_max(a):
    return jnp.max(a, axis=1, keepdims=True)


def row_sum(a):
    return jnp.sum(a, axis=1, keepdims=True)


def shape(*dims, dtype=BF16):
    return jax.ShapeDtypeStruct(dims, dtype)


def call(body, out_shape, specs, scratch=()):
    return pl.pallas_call(
        body,
        out_shape=out_shape,
        in_specs=specs,
        out_specs=jax.tree.map(lambda _: VMEM, out_shape),
        scratch_shapes=list(scratch),
        compiler_params=PARAMS,
    )


def coord(name):
    return lax.axis_index(name).astype(jnp.int32)


def my_residue():
    return coord("x") * 4 + coord("c") * 2 + coord("h")


def pack_body(*refs):
    out_ref = refs[-1]
    for i, ref in enumerate(refs[:-1]):
        for d in range(HEADS):
            out_ref[d, i * ROWS : (i + 1) * ROWS, :] = ref[:, d * HD : (d + 1) * HD]


def pack(*arrays):
    return call(pack_body, shape(HEADS, 4 * ROWS, HD), [VMEM] * 4)(*arrays)


def unpack_body(x_ref, *refs):
    for i, ref in enumerate(refs):
        for d in range(HEADS):
            ref[:, d * HD : (d + 1) * HD] = x_ref[d, i * ROWS : (i + 1) * ROWS, :]


def unpack(x):
    return call(unpack_body, (shape(ROWS, HEADS * HD),) * 2, [VMEM])(x)


Q, K, V, G = range(4)


def block_of(ref, zz, a):
    return ref[4 * zz : 4 * zz + 4, a * ROWS : (a + 1) * ROWS, :].reshape(BLK, HD)


def summary_body(cols_ref, k_ref, v_ref, out_ref):
    block = coord("z") * 16 + my_residue()
    quarter = coord("q")
    row = lax.broadcasted_iota(jnp.int32, (8, ROWS), 0)
    lane = lax.broadcasted_iota(jnp.int32, (8, ROWS), 1)
    first = cols_ref[2 * quarter, block] - ROWS * quarter
    second = cols_ref[2 * quarter + 1, block] - ROWS * quarter
    hit = lane == jnp.where((row & 1) == 0, first, second)
    of_keys = (row & 2) == 0
    pick_k = (hit & of_keys).astype(F32).astype(BF16)
    pick_v = (hit & jnp.logical_not(of_keys)).astype(F32).astype(BF16)
    rows = dot_nn(pick_k, k_ref[...]) + dot_nn(pick_v, v_ref[...])
    upper = lax.broadcasted_iota(jnp.int32, (8, HD), 0) < 4
    for d in range(0, HEADS, 4):
        two = []
        for e in (d, d + 2):
            one = rows[:, e * HD : (e + 1) * HD]
            other = rows[:, (e + 1) * HD : (e + 2) * HD]
            two.append(jnp.where(upper, one, other))
        four = jnp.concatenate(two).astype(BF16)
        for h in range(2):
            at = (d // 4) * 32 + h * 16
            out_ref[at : at + 16, :] = four


def summary(cols, k, v):
    return call(summary_body, shape(8 * HEADS, HD), [SMEM, VMEM, VMEM])(cols, k, v)


def causal_mask():
    rows = lax.broadcasted_iota(jnp.int32, (BLK, BLK), 0)
    return rows >= lax.broadcasted_iota(jnp.int32, (BLK, BLK), 1)


def is_kept(run_ref, block):
    return (block < run_ref[0]) | (block >= run_ref[1])


def attend_blocks(blocks, causal):
    tops, own, far = [], [], []
    for q, k, _, _, _, (ks, _, bias) in blocks:
        own.append(jnp.where(causal, dot_nt(q, k) * LOG2, NEG))
        far.append(None if ks is None else dot_nt(q, ks) * LOG2 + bias)
    for i in range(len(blocks)):
        top = row_max(own[i])
        tops.append(top if far[i] is None else jnp.maximum(top, row_max(far[i])))
    invs = []
    for i, (_, _, _, _, alive, _) in enumerate(blocks):
        own[i] = jnp.exp2(own[i] - tops[i])
        total = row_sum(own[i])
        if far[i] is not None:
            far[i] = jnp.exp2(far[i] - tops[i])
            total = total + row_sum(far[i])
        invs.append(alive / total)
    low_own, low_far, outs = [], [], []
    for i, (_, _, v, _, _, (_, vs, _)) in enumerate(blocks):
        own[i] = own[i] * invs[i]
        low_own.append(own[i].astype(BF16))
        out = dot_nn(low_own[i], v)
        low_far.append(None)
        if far[i] is not None:
            far[i] = far[i] * invs[i]
            low_far[i] = far[i].astype(BF16)
            out = out + dot_nn(low_far[i], vs)
        outs.append(out.astype(BF16))
    deltas = [
        row_sum(g.astype(F32) * out.astype(F32)) for (_, _, _, g, _, _), out in zip(blocks, outs)
    ]
    results = []
    for i, (_, k, v, g, _, (ks, vs, _)) in enumerate(blocks):
        ds_own = (own[i] * (dot_nt(g, v) - deltas[i]) * SCALE).astype(BF16)
        dq = dot_nn(ds_own, k)
        ds_far = None
        if ks is not None:
            ds_far = (far[i] * (dot_nt(g, vs) - deltas[i]) * SCALE).astype(BF16)
            dq = dq + dot_nn(ds_far, ks)
        results.append((outs[i], dq, ds_own, low_own[i], ds_far, low_far[i]))
    return results


def store(ref, zz, a, rows):
    ref[4 * zz : 4 * zz + 4, a * ROWS : (a + 1) * ROWS, :] = rows.astype(BF16).reshape(4, ROWS, HD)


def rows_of(ref, low, high, a):
    count = (high - low) * BLK
    return ref[4 * low : 4 * high, a * ROWS : (a + 1) * ROWS, :].reshape(count, HD)


def fixed_head(run_ref, x_ref, parts, outs, out_ref, k_sc, v_sc, p_sc, d_sc):
    x, c = coord("x"), coord("c")
    residue = my_residue()
    causal = causal_mask()
    m = lax.broadcasted_iota(jnp.int32, (BLK, BLK), 0)
    source = ((m & 63) >> 3) * 16 + ((m & 7) >> 1) * 4 + (m >> 6) * 2 + (m & 1)
    order = (source == lax.broadcasted_iota(jnp.int32, (BLK, BLK), 1)).astype(F32).astype(BF16)
    for rel in range(16):
        base = ((rel >> 1) & 1) * 256 + (rel & 1) * 16
        mixed = jnp.concatenate(
            [parts[rel // 4][base + z * 32 : base + z * 32 + 16, :] for z in range(RUN)]
        )
        rows = dot_nn(order, mixed).astype(BF16)
        for pair in range(4):
            at = pair * 256 + rel * 16
            k_sc[at : at + 16, :] = rows[pair * 16 : (pair + 1) * 16, :]
            v_sc[at : at + 16, :] = rows[64 + pair * 16 : 64 + (pair + 1) * 16, :]
    n = lax.broadcasted_iota(jnp.int32, (1, 1024), 1)
    rel = (n >> 4) & 15
    of = (((x - (rel >> 2)) & 3) << 2) + ((c ^ ((rel >> 1) & 1)) << 1) + (rel & 1)
    col_block = (((n >> 8) * 2 + ((n >> 3) & 1)) << 4) + of
    kept = is_kept(run_ref, col_block)
    for first in range(0, RUN, SIDE):
        blocks = []
        for zz in range(first, first + SIDE):
            wide = (zz // 2 + 1) * 256
            current = zz * 16 + residue
            alive = jnp.where(is_kept(run_ref, current), 1.0, 0.0)
            bias = jnp.where((col_block < current) & kept, 0.0, NEG)[:, :wide]
            far = (k_sc[0:wide, :], v_sc[0:wide, :], bias)
            blocks.append([block_of(x_ref, zz, a) for a in (Q, K, V, G)] + [alive, far])
        for i, result in enumerate(attend_blocks(blocks, causal)):
            zz = first + i
            q, g, wide = blocks[i][0], blocks[i][3], (zz // 2 + 1) * 256
            out, dq, ds_own, low_own, ds_far, low_far = result
            store(out_ref, zz, 0, out)
            store(out_ref, zz, 1, dq)
            store(out_ref, zz, 2, dot_tn(ds_own, q))
            store(out_ref, zz, 3, dot_tn(low_own, g))
            p_sc[zz * BLK : (zz + 1) * BLK, 0:wide] = low_far
            d_sc[zz * BLK : (zz + 1) * BLK, 0:wide] = ds_far
    for pair in range(4):
        low = pair * 256
        dk = dot_tn(d_sc[low:, low : low + 256], rows_of(x_ref, 2 * pair, RUN, Q))
        dv = dot_tn(p_sc[low:, low : low + 256], rows_of(x_ref, 2 * pair, RUN, G))
        k_sc[low : low + 256, :] = dk.astype(BF16)
        v_sc[low : low + 256, :] = dv.astype(BF16)
    for rel in range(16):
        base = ((rel >> 1) & 1) * 256 + (rel & 1) * 16
        rows = jnp.concatenate(
            [
                ref[pair * 256 + rel * 16 : pair * 256 + rel * 16 + 16, :]
                for ref in (k_sc, v_sc)
                for pair in range(4)
            ]
        )
        mixed = dot_tn(order, rows).astype(BF16)
        for z in range(RUN):
            outs[rel // 4][base + z * 32 : base + z * 32 + 16, :] = mixed[z * 16 : (z + 1) * 16, :]


def strided_head(run_ref, pick_ref, x_ref, out_ref, sum_sc):
    residue = my_residue()
    causal = causal_mask()
    for start in range(0, RUN, SIDE):
        blocks = []
        for zz in range(start, start + SIDE):
            block = zz * 16 + residue
            count = min(zz, CANDS)
            alive = jnp.where(is_kept(run_ref, block), 1.0, 0.0)
            far = (None, None, None)
            if count:
                col = lax.broadcasted_iota(jnp.int32, (1, count * BLK), 1) >> 7
                bias = jnp.full((1, count * BLK), NEG, F32)
                for i in range(count):
                    m = count - i
                    picked = (pick_ref[0, block] == m) | (pick_ref[1, block] == m)
                    usable = picked & is_kept(run_ref, block - 16 * m)
                    bias = jnp.where(col == i, jnp.where(usable, 0.0, NEG), bias)
                far = tuple(rows_of(x_ref, zz - count, zz, a) for a in (K, V)) + (bias,)
            blocks.append([block_of(x_ref, zz, a) for a in (Q, K, V, G)] + [alive, far])
        for i, result in enumerate(attend_blocks(blocks, causal)):
            zz = start + i
            q, g, first = blocks[i][0], blocks[i][3], max(zz - CANDS, 0)
            out, dq, ds_own, low_own, ds_far, low_far = result
            store(out_ref, zz, 0, out)
            store(out_ref, zz, 1, dq)
            sum_sc[0, zz * BLK : (zz + 1) * BLK, :] = dot_tn(ds_own, q)
            sum_sc[1, zz * BLK : (zz + 1) * BLK, :] = dot_tn(low_own, g)
            if zz:
                sum_sc[0, first * BLK : zz * BLK, :] += dot_tn(ds_far, q)
                sum_sc[1, first * BLK : zz * BLK, :] += dot_tn(low_far, g)
    for zz in range(RUN):
        for a in range(2):
            store(out_ref, zz, 2 + a, sum_sc[a, zz * BLK : (zz + 1) * BLK, :])


def attend_body(run_ref, pick_ref, x_ref, s0, s1, s2, s3, *rest):
    out_ref, r0, r1, r2, r3, k_sc, v_sc, p_sc, d_sc, sum_sc = rest
    outs = (r0, r1, r2, r3)
    is_fixed = coord("q") < 2

    @pl.when(is_fixed)
    def _():
        fixed_head(run_ref, x_ref, (s0, s1, s2, s3), outs, out_ref, k_sc, v_sc, p_sc, d_sc)

    @pl.when(jnp.logical_not(is_fixed))
    def _():
        for ref in outs:
            ref[...] = jnp.zeros((512, HD), BF16)
        strided_head(run_ref, pick_ref, x_ref, out_ref, sum_sc)


def attend(run, pick, x, parts):
    outs = (shape(HEADS, 4 * ROWS, HD),) + (shape(512, HD),) * 4
    scratch = (
        [pltpu.VMEM((1024, HD), BF16)] * 2
        + [pltpu.VMEM((1024, 1024), BF16)] * 2
        + [pltpu.VMEM((2, 1024, HD), F32)]
    )
    return call(attend_body, outs, [SMEM, SMEM] + [VMEM] * 5, scratch)(run, pick, x, *parts)


def finish_body(cols_ref, x_ref, sum_ref, dk_ref, dv_ref):
    block = coord("z") * 16 + my_residue()
    quarter = coord("q")
    row = lax.broadcasted_iota(jnp.int32, (16, HD), 0)
    at = [cols_ref[2 * quarter + i, block] - ROWS * quarter - 16 * i for i in range(2)]
    for d in range(HEADS):
        lanes = slice(d * HD, (d + 1) * HD)
        if d % 4 >= 2:
            for a, ref in enumerate((dk_ref, dv_ref)):
                ref[:, lanes] = x_ref[d, (2 + a) * ROWS : (3 + a) * ROWS, :]
            continue
        if d % 4 == 0:
            base = (d // 4) * 32
            total = sum_ref[base : base + 16, :].astype(F32)
            total = total + sum_ref[base + 16 : base + 32, :].astype(F32)
        for a, ref in enumerate((dk_ref, dv_ref)):
            for i in range(2):
                n = (d % 4) * 4 + a * 2 + i
                extra = jnp.broadcast_to(total[n : n + 1, :], (16, HD))
                low = (2 + a) * ROWS + 16 * i
                own = x_ref[d, low : low + 16, :].astype(F32)
                value = own + jnp.where(row == at[i], extra, 0.0)
                ref[16 * i : 16 * i + 16, lanes] = value.astype(BF16)


def finish(cols, x, sums):
    return call(finish_body, (shape(ROWS, HEADS * HD),) * 2, [SMEM, VMEM, VMEM])(cols, x, sums)


def here(block):
    return pltpu.with_memory_space_constraint(block, pltpu.VMEM)


def exchange(block, axes):
    return lax.all_to_all(block, axes, split_axis=0, concat_axis=0, tiled=True)


def swap(block):
    return lax.ppermute(block, "c", [(0, 1), (1, 0)])


def turn(block, distance):
    return lax.ppermute(block, "x", [(i, (i + distance) % 4) for i in range(4)])


def gather_summaries(own):
    chip = jnp.concatenate([own, swap(own)])
    return [chip] + [turn(chip, d) for d in range(1, 4)]


def scatter_partials(partials):
    total = partials[0].astype(F32)
    for d in range(1, 4):
        total = total + turn(partials[d], -d).astype(F32)
    half = total.shape[0] // 2
    total = total[:half] + swap(total[half:].astype(BF16)).astype(F32)
    return exchange(total.astype(BF16), OWNERS)


def shards(query, key_in, value, out_grad, block_keep, strided_pick, summary_cols):
    cols = summary_cols.T
    ids = jnp.arange(block_keep.shape[0], dtype=jnp.int32)
    removed = block_keep != 1
    gone = jnp.min(jnp.where(removed, ids, ids.shape[0]))
    run = jnp.stack([gone, jnp.max(jnp.where(removed, ids + 1, 0))])
    own = exchange(summary(cols, key_in, value), OWNERS)
    send, own = lax.optimization_barrier((pack(query, key_in, value, out_grad), own))
    got = exchange(send, GROUP)
    parts = [here(part) for part in gather_summaries(own)]
    outs, *partials = attend(run, strided_pick.T, here(got), parts)
    back = exchange(outs, GROUP)
    sums = scatter_partials(partials)
    back = here(back)
    return tuple(unpack(back)) + tuple(finish(cols, back, here(sums)))


def solution(mesh):
    split = Mesh(np.asarray(mesh.devices).reshape(8, 4, 2, 2, 4), AXES)
    tokens = P(AXES, None)
    return jax.shard_map(
        shards,
        mesh=split,
        in_specs=(tokens, tokens, tokens, tokens, P(), P(), P()),
        out_specs=(tokens, tokens, tokens, tokens),
        check_vma=False,
    )
```

```python
import math

import jax
import jax.numpy as jnp
import numpy as np
from jax import lax
from jax.experimental import pallas as pl
from jax.experimental.pallas import tpu as pltpu
from jax.sharding import Mesh
from jax.sharding import PartitionSpec as P

HD = 128
BLK = 128
CANDS = 4
ROWS = 32
HEADS = 32
RUN = 8
SIDE = 8
SCALE = 1.0 / math.sqrt(HD)
LOG2 = SCALE * math.log2(math.e)
NEG = -1e30

AXES = ("z", "x", "c", "h", "q")
GROUP = ("z", "q")

F32 = jnp.float32
BF16 = jnp.bfloat16

VMEM = pl.BlockSpec(memory_space=pltpu.VMEM)
SMEM = pl.BlockSpec(memory_space=pltpu.SMEM)
PARAMS = pltpu.CompilerParams(vmem_limit_bytes=56 * 1024 * 1024)


def dot(a, b, dims):
    return lax.dot_general(a, b, (dims, ((), ())), preferred_element_type=F32)


def dot_nt(a, b):
    return dot(a, b, ((1,), (1,)))


def dot_nn(a, b):
    return dot(a, b, ((1,), (0,)))


def dot_tn(a, b):
    return dot(a, b, ((0,), (0,)))


def row_max(a):
    return jnp.max(a, axis=1, keepdims=True)


def row_sum(a):
    return jnp.sum(a, axis=1, keepdims=True)


def shape(*dims, dtype=BF16):
    return jax.ShapeDtypeStruct(dims, dtype)


def call(body, out_shape, specs, scratch=()):
    return pl.pallas_call(
        body,
        out_shape=out_shape,
        in_specs=specs,
        out_specs=jax.tree.map(lambda _: VMEM, out_shape),
        scratch_shapes=list(scratch),
        compiler_params=PARAMS,
    )


def coord(name):
    return lax.axis_index(name).astype(jnp.int32)


def my_residue():
    return coord("x") * 4 + coord("c") * 2 + coord("h")


def pack_body(*refs):
    out_ref = refs[-1]
    for i, ref in enumerate(refs[:-1]):
        for d in range(HEADS):
            out_ref[d, i * ROWS : (i + 1) * ROWS, :] = ref[:, d * HD : (d + 1) * HD]


def pack(*arrays):
    return call(pack_body, shape(HEADS, 4 * ROWS, HD), [VMEM] * 4)(*arrays)


def unpack_body(x_ref, *refs):
    for i, ref in enumerate(refs):
        for d in range(HEADS):
            ref[:, d * HD : (d + 1) * HD] = x_ref[d, i * ROWS : (i + 1) * ROWS, :]


def unpack(x):
    return call(unpack_body, (shape(ROWS, HEADS * HD),) * 2, [VMEM])(x)


Q, K, V, G = range(4)


def block_of(ref, zz, a):
    return ref[4 * zz : 4 * zz + 4, a * ROWS : (a + 1) * ROWS, :].reshape(BLK, HD)


def summary_body(cols_ref, k_ref, v_ref, out_ref):
    block = coord("z") * 16 + my_residue()
    quarter = coord("q")
    row = lax.broadcasted_iota(jnp.int32, (8, ROWS), 0)
    lane = lax.broadcasted_iota(jnp.int32, (8, ROWS), 1)
    first = cols_ref[2 * quarter, block] - ROWS * quarter
    second = cols_ref[2 * quarter + 1, block] - ROWS * quarter
    hit = lane == jnp.where((row & 1) == 0, first, second)
    of_keys = (row & 2) == 0
    pick_k = (hit & of_keys).astype(F32).astype(BF16)
    pick_v = (hit & jnp.logical_not(of_keys)).astype(F32).astype(BF16)
    rows = dot_nn(pick_k, k_ref[...]) + dot_nn(pick_v, v_ref[...])
    upper = lax.broadcasted_iota(jnp.int32, (8, HD), 0) < 4
    for d in range(0, HEADS, 4):
        two = []
        for e in (d, d + 2):
            one = rows[:, e * HD : (e + 1) * HD]
            other = rows[:, (e + 1) * HD : (e + 2) * HD]
            two.append(jnp.where(upper, one, other))
        four = jnp.concatenate(two).astype(BF16)
        out_ref[4 * d : 4 * d + 16, :] = four


def summary(cols, k, v):
    return call(summary_body, shape(4 * HEADS, HD), [SMEM, VMEM, VMEM])(cols, k, v)


def causal_mask():
    rows = lax.broadcasted_iota(jnp.int32, (BLK, BLK), 0)
    return rows >= lax.broadcasted_iota(jnp.int32, (BLK, BLK), 1)


def is_kept(run_ref, block):
    return (block < run_ref[0]) | (block >= run_ref[1])


def attend_blocks(blocks, causal):
    tops, own, far = [], [], []
    for q, k, _, _, _, (ks, _, bias) in blocks:
        own.append(jnp.where(causal, dot_nt(q, k) * LOG2, NEG))
        far.append(None if ks is None else dot_nt(q, ks) * LOG2 + bias)
    for i in range(len(blocks)):
        top = row_max(own[i])
        tops.append(top if far[i] is None else jnp.maximum(top, row_max(far[i])))
    invs = []
    for i, (_, _, _, _, alive, _) in enumerate(blocks):
        own[i] = jnp.exp2(own[i] - tops[i])
        total = row_sum(own[i])
        if far[i] is not None:
            far[i] = jnp.exp2(far[i] - tops[i])
            total = total + row_sum(far[i])
        invs.append(alive / total)
    low_own, low_far, outs = [], [], []
    for i, (_, _, v, _, _, (_, vs, _)) in enumerate(blocks):
        own[i] = own[i] * invs[i]
        low_own.append(own[i].astype(BF16))
        out = dot_nn(low_own[i], v)
        low_far.append(None)
        if far[i] is not None:
            far[i] = far[i] * invs[i]
            low_far[i] = far[i].astype(BF16)
            out = out + dot_nn(low_far[i], vs)
        outs.append(out.astype(BF16))
    deltas = [
        row_sum(g.astype(F32) * out.astype(F32)) for (_, _, _, g, _, _), out in zip(blocks, outs)
    ]
    results = []
    for i, (_, k, v, g, _, (ks, vs, _)) in enumerate(blocks):
        ds_own = (own[i] * (dot_nt(g, v) - deltas[i]) * SCALE).astype(BF16)
        dq = dot_nn(ds_own, k)
        ds_far = None
        if ks is not None:
            ds_far = (far[i] * (dot_nt(g, vs) - deltas[i]) * SCALE).astype(BF16)
            dq = dq + dot_nn(ds_far, ks)
        results.append((outs[i], dq, ds_own, low_own[i], ds_far, low_far[i]))
    return results


def store(ref, zz, a, rows):
    ref[4 * zz : 4 * zz + 4, a * ROWS : (a + 1) * ROWS, :] = rows.astype(BF16).reshape(4, ROWS, HD)


def rows_of(ref, low, high, a):
    count = (high - low) * BLK
    return ref[4 * low : 4 * high, a * ROWS : (a + 1) * ROWS, :].reshape(count, HD)


def fixed_head(run_ref, x_ref, parts, outs, out_ref, k_sc, v_sc, p_sc, d_sc):
    x, c, h = coord("x"), coord("c"), coord("h")
    residue = my_residue()
    causal = causal_mask()
    m = lax.broadcasted_iota(jnp.int32, (BLK, BLK), 0)
    source = ((m & 63) >> 3) * 16 + ((m & 7) >> 1) * 4 + (m >> 6) * 2 + (m & 1)
    order = (source == lax.broadcasted_iota(jnp.int32, (BLK, BLK), 1)).astype(F32).astype(BF16)
    for rel in range(16):
        base = (rel % 4) * BLK
        mixed = parts[rel // 4][base : base + BLK, :]
        rows = dot_nn(order, mixed).astype(BF16)
        for pair in range(4):
            at = pair * 256 + rel * 16
            k_sc[at : at + 16, :] = rows[pair * 16 : (pair + 1) * 16, :]
            v_sc[at : at + 16, :] = rows[64 + pair * 16 : 64 + (pair + 1) * 16, :]
    n = lax.broadcasted_iota(jnp.int32, (1, 1024), 1)
    rel = (n >> 4) & 15
    of = (((x - (rel >> 2)) & 3) << 2) + ((c ^ ((rel >> 1) & 1)) << 1) + (h ^ (rel & 1))
    col_block = (((n >> 8) * 2 + ((n >> 3) & 1)) << 4) + of
    kept = is_kept(run_ref, col_block)
    for first in range(0, RUN, SIDE):
        blocks = []
        for zz in range(first, first + SIDE):
            wide = (zz // 2 + 1) * 256
            current = zz * 16 + residue
            alive = jnp.where(is_kept(run_ref, current), 1.0, 0.0)
            bias = jnp.where((col_block < current) & kept, 0.0, NEG)[:, :wide]
            far = (k_sc[0:wide, :], v_sc[0:wide, :], bias)
            blocks.append([block_of(x_ref, zz, a) for a in (Q, K, V, G)] + [alive, far])
        for i, result in enumerate(attend_blocks(blocks, causal)):
            zz = first + i
            q, g, wide = blocks[i][0], blocks[i][3], (zz // 2 + 1) * 256
            out, dq, ds_own, low_own, ds_far, low_far = result
            store(out_ref, zz, 0, out)
            store(out_ref, zz, 1, dq)
            store(out_ref, zz, 2, dot_tn(ds_own, q))
            store(out_ref, zz, 3, dot_tn(low_own, g))
            p_sc[zz * BLK : (zz + 1) * BLK, 0:wide] = low_far
            d_sc[zz * BLK : (zz + 1) * BLK, 0:wide] = ds_far
    for pair in range(4):
        low = pair * 256
        dk = dot_tn(d_sc[low:, low : low + 256], rows_of(x_ref, 2 * pair, RUN, Q))
        dv = dot_tn(p_sc[low:, low : low + 256], rows_of(x_ref, 2 * pair, RUN, G))
        k_sc[low : low + 256, :] = dk.astype(BF16)
        v_sc[low : low + 256, :] = dv.astype(BF16)
    for rel in range(16):
        base = (rel % 4) * BLK
        rows = jnp.concatenate(
            [
                ref[pair * 256 + rel * 16 : pair * 256 + rel * 16 + 16, :]
                for ref in (k_sc, v_sc)
                for pair in range(4)
            ]
        )
        outs[rel // 4][base : base + BLK, :] = dot_tn(order, rows).astype(BF16)


def strided_head(run_ref, pick_ref, x_ref, out_ref, sum_sc):
    residue = my_residue()
    causal = causal_mask()
    for start in range(0, RUN, SIDE):
        blocks = []
        for zz in range(start, start + SIDE):
            block = zz * 16 + residue
            count = min(zz, CANDS)
            alive = jnp.where(is_kept(run_ref, block), 1.0, 0.0)
            far = (None, None, None)
            if count:
                col = lax.broadcasted_iota(jnp.int32, (1, count * BLK), 1) >> 7
                bias = jnp.full((1, count * BLK), NEG, F32)
                for i in range(count):
                    m = count - i
                    picked = (pick_ref[0, block] == m) | (pick_ref[1, block] == m)
                    usable = picked & is_kept(run_ref, block - 16 * m)
                    bias = jnp.where(col == i, jnp.where(usable, 0.0, NEG), bias)
                far = tuple(rows_of(x_ref, zz - count, zz, a) for a in (K, V)) + (bias,)
            blocks.append([block_of(x_ref, zz, a) for a in (Q, K, V, G)] + [alive, far])
        for i, result in enumerate(attend_blocks(blocks, causal)):
            zz = start + i
            q, g, first = blocks[i][0], blocks[i][3], max(zz - CANDS, 0)
            out, dq, ds_own, low_own, ds_far, low_far = result
            store(out_ref, zz, 0, out)
            store(out_ref, zz, 1, dq)
            sum_sc[0, zz * BLK : (zz + 1) * BLK, :] = dot_tn(ds_own, q)
            sum_sc[1, zz * BLK : (zz + 1) * BLK, :] = dot_tn(low_own, g)
            if zz:
                sum_sc[0, first * BLK : zz * BLK, :] += dot_tn(ds_far, q)
                sum_sc[1, first * BLK : zz * BLK, :] += dot_tn(low_far, g)
    for zz in range(RUN):
        for a in range(2):
            store(out_ref, zz, 2 + a, sum_sc[a, zz * BLK : (zz + 1) * BLK, :])


def attend_body(run_ref, pick_ref, x_ref, s0, s1, s2, s3, *rest):
    out_ref, r0, r1, r2, r3, k_sc, v_sc, p_sc, d_sc, sum_sc = rest
    outs = (r0, r1, r2, r3)
    is_fixed = coord("q") < 2

    @pl.when(is_fixed)
    def _():
        fixed_head(run_ref, x_ref, (s0, s1, s2, s3), outs, out_ref, k_sc, v_sc, p_sc, d_sc)

    @pl.when(jnp.logical_not(is_fixed))
    def _():
        for ref in outs:
            ref[...] = jnp.zeros((512, HD), BF16)
        strided_head(run_ref, pick_ref, x_ref, out_ref, sum_sc)


def attend(run, pick, x, parts):
    outs = (shape(HEADS, 4 * ROWS, HD),) + (shape(512, HD),) * 4
    scratch = (
        [pltpu.VMEM((1024, HD), BF16)] * 2
        + [pltpu.VMEM((1024, 1024), BF16)] * 2
        + [pltpu.VMEM((2, 1024, HD), F32)]
    )
    return call(attend_body, outs, [SMEM, SMEM] + [VMEM] * 5, scratch)(run, pick, x, *parts)


def finish_body(cols_ref, x_ref, sum_ref, dk_ref, dv_ref):
    block = coord("z") * 16 + my_residue()
    quarter = coord("q")
    row = lax.broadcasted_iota(jnp.int32, (16, HD), 0)
    at = [cols_ref[2 * quarter + i, block] - ROWS * quarter - 16 * i for i in range(2)]
    for d in range(HEADS):
        lanes = slice(d * HD, (d + 1) * HD)
        if d % 4 >= 2:
            for a, ref in enumerate((dk_ref, dv_ref)):
                ref[:, lanes] = x_ref[d, (2 + a) * ROWS : (3 + a) * ROWS, :]
            continue
        if d % 4 == 0:
            total = sum_ref[4 * d : 4 * d + 16, :].astype(F32)
        for a, ref in enumerate((dk_ref, dv_ref)):
            for i in range(2):
                n = (d % 4) * 4 + a * 2 + i
                extra = jnp.broadcast_to(total[n : n + 1, :], (16, HD))
                low = (2 + a) * ROWS + 16 * i
                own = x_ref[d, low : low + 16, :].astype(F32)
                value = own + jnp.where(row == at[i], extra, 0.0)
                ref[16 * i : 16 * i + 16, lanes] = value.astype(BF16)


def finish(cols, x, sums):
    return call(finish_body, (shape(ROWS, HEADS * HD),) * 2, [SMEM, VMEM, VMEM])(cols, x, sums)


def here(block):
    return pltpu.with_memory_space_constraint(block, pltpu.VMEM)


def exchange(block, axes):
    return lax.all_to_all(block, axes, split_axis=0, concat_axis=0, tiled=True)


def swap(block, axis):
    return lax.ppermute(block, axis, [(0, 1), (1, 0)])


def turn(block, distance):
    return lax.ppermute(block, "x", [(i, (i + distance) % 4) for i in range(4)])


def gather_summaries(own):
    chip = own
    for axis in ("h", "c"):
        chip = jnp.concatenate([chip, swap(chip, axis)])
    return [chip] + [turn(chip, d) for d in range(1, 4)]


def scatter_partials(partials):
    total = partials[0].astype(F32)
    for d in range(1, 4):
        total = total + turn(partials[d], -d).astype(F32)
    for axis in ("c", "h"):
        half = total.shape[0] // 2
        total = total[:half] + swap(total[half:].astype(BF16), axis).astype(F32)
    return exchange(total.astype(BF16), GROUP)


def shards(query, key_in, value, out_grad, block_keep, strided_pick, summary_cols):
    cols = summary_cols.T
    ids = jnp.arange(block_keep.shape[0], dtype=jnp.int32)
    removed = block_keep != 1
    gone = jnp.min(jnp.where(removed, ids, ids.shape[0]))
    run = jnp.stack([gone, jnp.max(jnp.where(removed, ids + 1, 0))])
    own = exchange(summary(cols, key_in, value), GROUP)
    send, own = lax.optimization_barrier((pack(query, key_in, value, out_grad), own))
    got = exchange(send, GROUP)
    parts = [here(part) for part in gather_summaries(own)]
    outs, *partials = attend(run, strided_pick.T, here(got), parts)
    back = exchange(outs, GROUP)
    sums = scatter_partials(partials)
    back = here(back)
    return tuple(unpack(back)) + tuple(finish(cols, back, here(sums)))


def solution(mesh):
    split = Mesh(np.asarray(mesh.devices).reshape(8, 4, 2, 2, 4), AXES)
    tokens = P(AXES, None)
    return jax.shard_map(
        shards,
        mesh=split,
        in_specs=(tokens, tokens, tokens, tokens, P(), P(), P()),
        out_specs=(tokens, tokens, tokens, tokens),
        check_vma=False,
    )
```
